32 devices in a mesh: groups: 2 (over x), ep: 16 (over z, y, core).
Axes of the slice: x: 2, y: 2, z: 4, core: 2. Of those that a mesh axis runs over, the one named last changes fastest.
Arguments:
- tokens: bfloat16 [1024, 3584], P(('groups', 'ep')), parts along dimension 0, may hold values from -6 to 6
- routes: int32 [1024, 8], P(('groups', 'ep')), parts along dimension 0, may hold values from 0 to 255, all different within a row; in each aligned block of 32 rows (0 to 31, 32 to 63, ...) at most 2 rows name the same one
- gate_num: int32 [1024, 8], P(('groups', 'ep')), parts along dimension 0, may hold values from 1 to 255
- w_gate: bfloat16 [16, 3584, 512], P('ep'), may hold values from -0.09375 to 0.09375
- w_up: bfloat16 [16, 3584, 512], P('ep'), may hold values from -0.09375 to 0.09375
- w_down: bfloat16 [16, 512, 3584], P('ep'), may hold values from -0.1875 to 0.1875
Outputs:
- combined: bfloat16 [1024, 3584], P(('groups', 'ep')), parts along dimension 0
The draws below stay inside these ranges and needn't reach their ends.
There are 2 independent parts, one for each index of `groups`. The reference program is written for one: setup_inputs(seed, part) draws one part's arguments, and reference() takes and returns one part's arrays. A program takes and returns all parts, laid end to end along the dimension named above; an argument that names none is the same for every part. Nothing has to cross between parts.
Inputs may be any that keep to these rules, and one draw needn't show every extreme that they name: `routes`: each row names 8 different experts; among the 32 rows of one device no expert is named more than 2 times, a bound that some block reaches.
All inputs are finite; a program needn't handle non-finite values.
Results may differ from the reference program's by a relative error of at most 0.0058.
Values may be sent and summed in bfloat16 or wider, within the bound.
No kernel may reach another device: no remote copies, remote signals or barrier semaphores. Data moves between devices by JAX's collectives and lax.ppermute only.
A program may use at most 64 MiB of HBM per device.

```python
import math
import jax
import jax.numpy as jnp
import numpy as np
from jax import lax

D = 3584
FF = 1024
SPLIT = 2
FF_DEV = 512
TOPK = 8
EXPERTS = 256
TOK_DEV = 32
HELD = 8
TOKENS = 512
CAP = 2
N_EP = 16


def with_ends(drawn, rng, least, largest):
    shape = drawn.shape
    spot = [jax.random.randint(jax.random.fold_in(rng, axis), (), 0, shape[axis]) for axis in range(len(shape))]
    drawn = drawn.at[tuple(spot)].set(least)
    longest = shape.index(max(shape))
    spot[longest] = (spot[longest] + 1) % shape[longest]
    return drawn.at[tuple(spot)].set(largest)


def levels(stream_key, dims, pieces, least, high):
    loudness, own = 1.0, jax.random.fold_in(stream_key, 6)
    for dim, shards_of in pieces:
        steps = jnp.exp(jax.random.uniform(jax.random.fold_in(own, dim), (shards_of,), jnp.float32, least / len(pieces), high / len(pieces)))
        loudness = loudness * jnp.repeat(steps, dims[dim] // shards_of).reshape([-1 if axis == dim else 1 for axis in range(len(dims))])
    return loudness


def deal_out(rng, own, number, rows, amount, top, reach, slope):
    sequence = jax.random.permutation(rng, amount)
    crowded, common = load_shares(amount, rows * top, reach, slope, True), load_shares(amount, rows * top, reach, slope, False)
    places = jnp.arange(amount)

    def named(sizes, turn):
        used = int((sizes > 0).sum())
        fixed = max(1, used // 4)
        moved = fixed + (places - fixed + turn * (used - fixed)) % max(1, amount - fixed)
        return jnp.zeros((amount,), jnp.int32).at[sequence[jnp.where(places < fixed, places, moved)]].set(jnp.asarray(sizes, jnp.int32))

    sizes = jnp.where(number % 4 == 0, named(crowded, number // 4), named(common, number - number // 4 - 1))
    mixed = jax.random.permutation(jax.random.fold_in(own, 3), amount)
    giver, receiver = mixed[0:amount // 2 * 2:2], mixed[1:amount // 2 * 2:2]
    margin = jnp.minimum(sizes[giver] - 1, reach - sizes[receiver]) // 2
    margin = jnp.where((giver == sequence[0]) | (receiver == sequence[0]) | (sizes[receiver] == 0), 0, jnp.maximum(margin, 0))
    moved = jax.random.randint(jax.random.fold_in(own, 4), (amount // 2,), 0, 1 << 20) % (margin + 1)
    sizes = sizes.at[giver].add(-moved).at[receiver].add(moved)
    labels = jnp.searchsorted(jnp.cumsum(sizes), jnp.arange(rows * top), side="right").astype(jnp.int32)
    listing = labels.reshape(top, rows).T
    listing = listing[jax.random.permutation(jax.random.fold_in(own, 1), rows)]
    turn = jax.random.randint(jax.random.fold_in(own, 2), (rows, 1), 0, top)
    return jnp.take_along_axis(listing, (jnp.arange(top)[None, :] + turn) % top, axis=1)


def load_shares(amount, total, reach, skew, full):
    portions = [(1 << 20) // math.isqrt(rank ** skew) + 1 for rank in range(1, amount + 1)]
    largest = reach if full else min(reach, max(-(-total // amount), total * portions[0] // sum(portions)))
    least = 1 if total - largest >= amount - 1 else 0
    holding, surplus = [largest] + [least] * (amount - 1), total - largest - least * (amount - 1)
    while surplus > 0:
        movable = [i for i in range(1, amount) if holding[i] < largest] or [i for i in range(1, amount) if holding[i] < reach]
        whole, left = sum([portions[i] for i in movable]), surplus
        for i in movable:
            extra = min(reach - holding[i], max(1, left * portions[i] // whole), surplus)
            holding[i] = holding[i] + extra
            surplus = surplus - extra
    return np.array(holding)


def gaussian(key, extent, spread, limit, cuts=(), held_as=jnp.bfloat16):
    entries = spread * jax.random.normal(key, extent, jnp.float32)
    if cuts:
        entries = entries * levels(key, extent, cuts, -0.22, 0.18)
    return jnp.clip(entries, -limit, limit).astype(held_as)


def setup_inputs(seed: int = 0, part: int = 0) -> dict:
    key_of = jax.random.split(jax.random.key(seed), 7)
    own_keys = jax.random.split(jax.random.fold_in(key_of[6], part), 7)
    tokens = gaussian(own_keys[0], (TOKENS, D), 1.0, 6.0, ((0, 16),))
    routes_keys = jax.random.split(jax.random.fold_in(own_keys[1], 1), TOKENS // TOK_DEV)
    routes_turns = jax.random.permutation(jax.random.fold_in(own_keys[1], 3), TOKENS // TOK_DEV)
    routes = jax.vmap(lambda own, number: deal_out(jax.random.fold_in(own_keys[1], 2), own, number, TOK_DEV, EXPERTS, TOPK, CAP, 2))(routes_keys, routes_turns).reshape((TOKENS, TOPK))
    gate_num = with_ends(jax.random.randint(own_keys[2], (TOKENS, TOPK), 1, 256), jax.random.fold_in(own_keys[2], 1), 1, 255).astype(jnp.int32)
    w_gate = gaussian(key_of[3], (HELD * SPLIT, D, FF_DEV), D ** -0.5, 0.09375, ((0, 16),))
    w_up = gaussian(key_of[4], (HELD * SPLIT, D, FF_DEV), D ** -0.5, 0.09375, ((0, 16),))
    w_down = gaussian(key_of[5], (HELD * SPLIT, FF_DEV, D), FF ** -0.5, 0.1875, ((0, 16),))
    return dict(tokens=tokens, routes=routes, gate_num=gate_num, w_gate=w_gate, w_up=w_up, w_down=w_down)


def reference(tokens, routes, gate_num, w_gate, w_up, w_down):
    tok_total, top_count = routes.shape
    feature_width = tokens.shape[1]
    slot_total = N_EP * CAP
    expert_total = w_gate.shape[0] // SPLIT
    flat_routes = routes.reshape(-1).astype(jnp.int32)
    flat_gates = gate_num.reshape(-1).astype(jnp.float32) / 256.0
    gate_all = w_gate.reshape(expert_total, SPLIT, feature_width, w_gate.shape[2])
    up_all = w_up.reshape(expert_total, SPLIT, feature_width, w_up.shape[2])
    down_all = w_down.reshape(expert_total, SPLIT, w_down.shape[1], feature_width)

    def per_expert(combined, inputs):
        expert_id, gate_w, up_w, down_w = inputs
        chosen = flat_routes == expert_id
        slot_index = jnp.nonzero(chosen, size=slot_total, fill_value=0)[0].astype(jnp.int32)
        is_valid = jnp.arange(slot_total, dtype=jnp.int32) < jnp.sum(chosen.astype(jnp.int32))
        token_ids = slot_index // top_count
        row_block = jnp.where(is_valid[:, None], tokens[token_ids], jnp.zeros((), tokens.dtype))
        gate_scale = jnp.where(is_valid, flat_gates[slot_index], jnp.zeros((), jnp.float32))
        partial_value = jnp.zeros((slot_total, feature_width), jnp.float32)
        for piece in range(SPLIT):
            gate_part = jnp.dot(row_block, gate_w[piece], preferred_element_type=jnp.float32)
            up_part = jnp.dot(row_block, up_w[piece], preferred_element_type=jnp.float32)
            hidden = (jax.nn.silu(gate_part) * up_part).astype(jnp.bfloat16)
            partial_value = partial_value + jnp.dot(hidden, down_w[piece], preferred_element_type=jnp.float32)
        output = partial_value.astype(jnp.bfloat16)
        total = gate_scale[:, None] * output.astype(jnp.float32)
        combined = combined.at[token_ids].add(total)
        return combined, None

    start = jnp.zeros((tok_total, feature_width), jnp.float32)
    expert_ids = jnp.arange(expert_total, dtype=jnp.int32)
    combined, unused = lax.scan(per_expert, start, (expert_ids, gate_all, up_all, down_all))
    return combined.astype(jnp.bfloat16)
```

```python
import functools
import jax
import jax.numpy as jnp
from jax import lax
from jax.experimental import pallas as pl
from jax.experimental.pallas import tpu as pltpu
from jax.sharding import PartitionSpec as P

SPLIT = 2
EXPERTS = 256


def choose(routes, gates, slots, capacity):
    rows, top = routes.shape
    slot = lax.broadcasted_iota(jnp.int32, (rows, slots), 1)
    expert, place = slot // capacity, slot % capacity
    hit = jnp.zeros((rows, slots), jnp.float32)
    gate = jnp.zeros((rows, slots), jnp.float32)
    for k in range(top):
        same = routes[:, k : k + 1] == expert
        hit = jnp.where(same, 1.0, hit)
        gate = jnp.where(same, gates[:, k : k + 1].astype(jnp.float32) / 256.0, gate)
    earlier = lax.broadcasted_iota(jnp.int32, (rows, rows), 0) > lax.broadcasted_iota(
        jnp.int32, (rows, rows), 1
    )
    rank = jnp.dot(
        earlier.astype(jnp.bfloat16), hit.astype(jnp.bfloat16), preferred_element_type=jnp.float32
    )
    mine = rank == place.astype(jnp.float32)
    return jnp.where(mine, hit, 0.0).astype(jnp.bfloat16), jnp.where(mine, gate, 0.0).astype(
        jnp.bfloat16
    )


def route_kernel(capacity, routes_ref, gates_ref, tokens_ref, out_ref, weight_ref):
    chips = out_ref.shape[0]
    pick, weight = choose(routes_ref[...], gates_ref[...], chips * capacity, capacity)
    weight_ref[...] = weight
    rows = lax.dot_general(
        pick, tokens_ref[...], (((0,), (0,)), ((), ())), preferred_element_type=jnp.float32
    ).astype(jnp.bfloat16)
    out_ref[...] = rows.reshape(out_ref.shape)


def mlp_kernel(own_ref, other_ref, gate_ref, up_ref, down_ref, keep_ref, send_ref):
    shape = own_ref.shape
    flat = (shape[0] * shape[1], shape[2])
    x = jnp.concatenate([own_ref[...].reshape(flat), other_ref[...].reshape(flat)], axis=0)
    gate = jnp.dot(x, gate_ref[0], preferred_element_type=jnp.float32)
    up = jnp.dot(x, up_ref[0], preferred_element_type=jnp.float32)
    hidden = (gate / (1.0 + jnp.exp(-gate)) * up).astype(jnp.bfloat16)
    out = jnp.dot(hidden, down_ref[0], preferred_element_type=jnp.float32)
    keep_ref[...] = out[: flat[0]].reshape(shape)
    send_ref[...] = out[flat[0] :].astype(jnp.bfloat16).reshape(shape)


def combine_kernel(weight_ref, rows_ref, out_ref):
    shape = rows_ref.shape
    rows = rows_ref[...].reshape(shape[0] * shape[1], shape[2])
    out_ref[...] = jnp.dot(weight_ref[...], rows, preferred_element_type=jnp.float32).astype(
        jnp.bfloat16
    )


VMEM = pl.BlockSpec(memory_space=pltpu.VMEM)
LIMIT = pltpu.CompilerParams(vmem_limit_bytes=16 << 20)


def shards(tokens, routes, gate_num, w_gate, w_up, w_down):
    tok_rows, top_count = routes.shape
    width = tokens.shape[1]
    devices = lax.axis_size("ep")
    chips = devices // SPLIT
    capacity = max(2, min(tok_rows, 5 * tok_rows * top_count // (2 * EXPERTS)))
    same_core = [[c * SPLIT + k for c in range(chips)] for k in range(SPLIT)]
    swap = [(d, d ^ 1) for d in range(devices)]
    block = (chips, capacity, width)
    outgoing, weight = pl.pallas_call(
        functools.partial(route_kernel, capacity),
        out_shape=(
            jax.ShapeDtypeStruct(block, jnp.bfloat16),
            jax.ShapeDtypeStruct((tok_rows, chips * capacity), jnp.bfloat16),
        ),
        in_specs=[VMEM] * 3,
        out_specs=(VMEM, VMEM),
        name="route",
        cost_estimate=pl.CostEstimate(flops=10**10, bytes_accessed=10**8, transcendentals=0),
        compiler_params=LIMIT,
    )(routes, gate_num, tokens)
    own = lax.all_to_all(
        outgoing, "ep", split_axis=0, concat_axis=0, tiled=True, axis_index_groups=same_core
    )
    other = lax.ppermute(own, "ep", swap)
    weights = [pltpu.with_memory_space_constraint(w, pltpu.VMEM) for w in (w_gate, w_up, w_down)]
    keep, send = pl.pallas_call(
        mlp_kernel,
        out_shape=(
            jax.ShapeDtypeStruct(block, jnp.float32),
            jax.ShapeDtypeStruct(block, jnp.bfloat16),
        ),
        in_specs=[VMEM] * 5,
        out_specs=(VMEM, VMEM),
        name="mlp",
        compiler_params=LIMIT,
    )(own, other, *weights)
    arrived = lax.ppermute(send, "ep", swap)
    summed = (keep + arrived.astype(jnp.float32)).astype(jnp.bfloat16)
    returned = lax.all_to_all(
        summed, "ep", split_axis=0, concat_axis=0, tiled=True, axis_index_groups=same_core
    )
    return pl.pallas_call(
        combine_kernel,
        out_shape=jax.ShapeDtypeStruct((tok_rows, width), jnp.bfloat16),
        in_specs=[VMEM] * 2,
        out_specs=VMEM,
        name="combine",
        compiler_params=LIMIT,
    )(weight, returned)


def solution(mesh):
    return jax.shard_map(
        shards,
        mesh=mesh,
        in_specs=(
            P(("groups", "ep"), None),
            P(("groups", "ep"), None),
            P(("groups", "ep"), None),
            P("ep", None, None),
            P("ep", None, None),
            P("ep", None, None),
        ),
        out_specs=P(("groups", "ep"), None),
        check_vma=False,
    )
```

```python
import functools
import jax
import jax.numpy as jnp
from jax import lax
from jax.experimental import pallas as pl
from jax.experimental.pallas import tpu as pltpu
from jax.sharding import PartitionSpec as P

SPLIT = 2
EXPERTS = 256


def slots_of(routes, slots, capacity, order):
    top, rows = routes.shape
    slot = lax.broadcasted_iota(jnp.int32, (slots, rows), 0)
    block, place = slot // capacity, slot % capacity
    expert = jnp.zeros_like(block)
    for j, chip in enumerate(order):
        expert = jnp.where(block == j, chip, expert)
    same = [routes[k : k + 1, :] == expert for k in range(top)]
    hit = functools.reduce(jnp.logical_or, same).astype(jnp.float32)
    earlier = lax.broadcasted_iota(jnp.int32, (rows, rows), 0) < lax.broadcasted_iota(
        jnp.int32, (rows, rows), 1
    )
    rank = jnp.dot(
        hit.astype(jnp.bfloat16), earlier.astype(jnp.bfloat16), preferred_element_type=jnp.float32
    )
    return jnp.where(rank == place.astype(jnp.float32), hit, 0.0), same


def route_kernel(capacity, order, routes_ref, gates_ref, tokens_ref, out_ref, weight_ref):
    chips = out_ref.shape[0]
    pick, same = slots_of(routes_ref[...], chips * capacity, capacity, order)
    rows = jnp.dot(
        pick.astype(jnp.bfloat16), tokens_ref[...], preferred_element_type=jnp.float32
    ).astype(jnp.bfloat16)
    out_ref[...] = rows.reshape(out_ref.shape)
    gates = gates_ref[...].astype(jnp.float32) / 256.0
    weight = jnp.zeros_like(pick)
    for k, chosen in enumerate(same):
        weight = jnp.where(chosen, gates[k : k + 1, :], weight)
    weight_ref[...] = (weight * pick).astype(jnp.bfloat16)


def mlp_kernel(own_ref, other_ref, gate_ref, up_ref, down_ref, keep_ref, send_ref):
    shape = own_ref.shape
    flat = (shape[0] * shape[1], shape[2])
    x = jnp.concatenate([own_ref[...].reshape(flat), other_ref[...].reshape(flat)], axis=0)
    gate = jnp.dot(x, gate_ref[0], preferred_element_type=jnp.float32)
    up = jnp.dot(x, up_ref[0], preferred_element_type=jnp.float32)
    hidden = (gate / (1.0 + jnp.exp(-gate)) * up).astype(jnp.bfloat16)
    out = jnp.dot(hidden, down_ref[0], preferred_element_type=jnp.float32)
    keep_ref[...] = out[: flat[0]].reshape(shape)
    send_ref[...] = out[flat[0] :].astype(jnp.bfloat16).reshape(shape)


def combine_kernel(weight_ref, rows_ref, out_ref):
    shape = rows_ref.shape
    rows = rows_ref[...].reshape(shape[0] * shape[1], shape[2])
    out_ref[...] = lax.dot_general(
        weight_ref[...], rows, (((0,), (0,)), ((), ())), preferred_element_type=jnp.float32
    ).astype(jnp.bfloat16)


def group_order(chips):
    first = (5 * chips) // 8
    return [first] + [c for c in range(chips) if c != first]


VMEM = pl.BlockSpec(memory_space=pltpu.VMEM)
WHOLE = pl.BlockSpec()
LIMIT = pltpu.CompilerParams(vmem_limit_bytes=16 << 20)


def shards(tokens, routes, gate_num, w_gate, w_up, w_down):
    tok_rows, top_count = routes.shape
    width = tokens.shape[1]
    devices = lax.axis_size("ep")
    chips = devices // SPLIT
    capacity = max(2, min(tok_rows, 5 * tok_rows * top_count // (2 * EXPERTS)))
    order = group_order(chips)
    same_core = [[c * SPLIT + k for c in order] for k in range(SPLIT)]
    swap = [(d, d ^ 1) for d in range(devices)]
    block = (chips, capacity, width)
    outgoing, weight = pl.pallas_call(
        functools.partial(route_kernel, capacity, order),
        out_shape=(
            jax.ShapeDtypeStruct(block, jnp.bfloat16),
            jax.ShapeDtypeStruct((chips * capacity, tok_rows), jnp.bfloat16),
        ),
        in_specs=[WHOLE] * 3,
        out_specs=(VMEM, VMEM),
        name="route",
        cost_estimate=pl.CostEstimate(flops=10**10, bytes_accessed=10**8, transcendentals=0),
        compiler_params=LIMIT,
    )(*(pltpu.with_memory_space_constraint(a, pltpu.HBM) for a in (routes.T, gate_num.T, tokens)))
    own = lax.all_to_all(
        outgoing, "ep", split_axis=0, concat_axis=0, tiled=True, axis_index_groups=same_core
    )
    other = lax.ppermute(own, "ep", swap)
    weights = [pltpu.with_memory_space_constraint(w, pltpu.VMEM) for w in (w_gate, w_up, w_down)]
    keep, send = pl.pallas_call(
        mlp_kernel,
        out_shape=(
            jax.ShapeDtypeStruct(block, jnp.float32),
            jax.ShapeDtypeStruct(block, jnp.bfloat16),
        ),
        in_specs=[VMEM] * 5,
        out_specs=(VMEM, VMEM),
        name="mlp",
        compiler_params=LIMIT,
    )(own, other, *weights)
    arrived = lax.ppermute(send, "ep", swap)
    summed = (keep + arrived.astype(jnp.float32)).astype(jnp.bfloat16)
    returned = lax.all_to_all(
        summed, "ep", split_axis=0, concat_axis=0, tiled=True, axis_index_groups=same_core
    )
    return pl.pallas_call(
        combine_kernel,
        out_shape=jax.ShapeDtypeStruct((tok_rows, width), jnp.bfloat16),
        in_specs=[VMEM] * 2,
        out_specs=VMEM,
        name="combine",
        compiler_params=LIMIT,
    )(weight, returned)


def solution(mesh):
    return jax.shard_map(
        shards,
        mesh=mesh,
        in_specs=(
            P(("groups", "ep"), None),
            P(("groups", "ep"), None),
            P(("groups", "ep"), None),
            P("ep", None, None),
            P("ep", None, None),
            P("ep", None, None),
        ),
        out_specs=P(("groups", "ep"), None),
        check_vma=False,
    )
```

```python
import functools
import jax
import jax.numpy as jnp
from jax import lax
from jax.experimental import pallas as pl
from jax.experimental.pallas import tpu as pltpu
from jax.sharding import PartitionSpec as P

SPLIT = 2
EXPERTS = 256


def slots_of(routes, slots, capacity, order):
    top, rows = routes.shape
    slot = lax.broadcasted_iota(jnp.int32, (slots, rows), 0)
    block, place = slot // capacity, slot % capacity
    expert = jnp.zeros_like(block)
    for j, chip in enumerate(order):
        expert = jnp.where(block == j, chip, expert)
    same = [routes[k : k + 1, :] == expert for k in range(top)]
    hit = functools.reduce(jnp.logical_or, same).astype(jnp.float32)
    earlier = lax.broadcasted_iota(jnp.int32, (rows, rows), 0) < lax.broadcasted_iota(
        jnp.int32, (rows, rows), 1
    )
    rank = jnp.dot(
        hit.astype(jnp.bfloat16), earlier.astype(jnp.bfloat16), preferred_element_type=jnp.float32
    )
    return jnp.where(rank == place.astype(jnp.float32), hit, 0.0), same


def route_kernel(
    capacity, order, routes_hbm, gates_hbm, tokens_hbm, out_ref, weight_ref, routes_v, gates_v, tokens_v, sems
):
    chips, halves, _, half = out_ref.shape
    parts = tokens_v.shape[0] // halves
    wide = half // parts
    routes_copy = pltpu.make_async_copy(routes_hbm, routes_v, sems.at[0])
    gates_copy = pltpu.make_async_copy(gates_hbm, gates_v, sems.at[1])
    token_copies = [
        pltpu.make_async_copy(tokens_hbm.at[:, pl.ds(i * wide, wide)], tokens_v.at[i], sems.at[2 + i])
        for i in range(halves * parts)
    ]
    routes_copy.start()
    for copy in token_copies:
        copy.start()
    gates_copy.start()
    routes_copy.wait()
    pick, same = slots_of(routes_v[...], chips * capacity, capacity, order)
    chosen = pick.astype(jnp.bfloat16)
    for i, copy in enumerate(token_copies):
        copy.wait()
        rows = jnp.dot(chosen, tokens_v[i], preferred_element_type=jnp.float32)
        part = slice(i % parts * wide, (i % parts + 1) * wide)
        out_ref[:, i // parts, :, part] = rows.astype(jnp.bfloat16).reshape(chips, capacity, wide)
    gates_copy.wait()
    gates = gates_v[...].astype(jnp.float32) / 256.0
    weight = jnp.zeros_like(pick)
    for k, hit in enumerate(same):
        weight = jnp.where(hit, gates[k : k + 1, :], weight)
    weight_ref[...] = (weight * pick).astype(jnp.bfloat16)


def flat(rows):
    return rows.reshape(rows.shape[0] * rows.shape[1], rows.shape[2])


def half_of(side, half):
    return pl.ds(pl.multiple_of(side * half, 128), half)


def enter_kernel(own_ref, gate_ref, up_ref, gate_out, up_out):
    half = own_ref.shape[2]
    mine = half_of(lax.axis_index("ep") % SPLIT, half)
    x = flat(own_ref[...])
    gate_out[...] = jnp.dot(x, gate_ref[0, mine, :], preferred_element_type=jnp.float32)
    up_out[...] = jnp.dot(x, up_ref[0, mine, :], preferred_element_type=jnp.float32)


def middle_kernel(other_ref, gate_acc, up_acc, gate_ref, up_ref, down_ref, hidden_ref, send_ref):
    half = other_ref.shape[2]
    theirs = half_of(1 - lax.axis_index("ep") % SPLIT, half)
    x = flat(other_ref[...])
    gate = gate_acc[...] + jnp.dot(x, gate_ref[0, theirs, :], preferred_element_type=jnp.float32)
    up = up_acc[...] + jnp.dot(x, up_ref[0, theirs, :], preferred_element_type=jnp.float32)
    hidden = (gate / (1.0 + jnp.exp(-gate)) * up).astype(jnp.bfloat16)
    hidden_ref[...] = hidden
    out = jnp.dot(hidden, down_ref[0, :, theirs], preferred_element_type=jnp.float32)
    send_ref[...] = out.astype(jnp.bfloat16).reshape(send_ref.shape)


def leave_kernel(hidden_ref, down_ref, keep_ref):
    half = keep_ref.shape[2]
    mine = half_of(lax.axis_index("ep") % SPLIT, half)
    out = jnp.dot(hidden_ref[...], down_ref[0, :, mine], preferred_element_type=jnp.float32)
    keep_ref[...] = out.reshape(keep_ref.shape)


def combine_kernel(weight_ref, rows_ref, out_hbm, out_v, sems):
    halves, half = rows_ref.shape[1], rows_ref.shape[3]
    parts = out_v.shape[0] // halves
    wide = half // parts
    copies = []
    for i in range(halves * parts):
        part = slice(i % parts * wide, (i % parts + 1) * wide)
        rows = flat(rows_ref[:, i // parts, :, part])
        out_v[i] = lax.dot_general(
            weight_ref[...], rows, (((0,), (0,)), ((), ())), preferred_element_type=jnp.float32
        ).astype(jnp.bfloat16)
        copies.append(
            pltpu.make_async_copy(out_v.at[i], out_hbm.at[:, pl.ds(i * wide, wide)], sems.at[i])
        )
        copies[-1].start()
    for copy in copies:
        copy.wait()


def group_order(chips):
    first = (5 * chips) // 8
    return [first] + [c for c in range(chips) if c != first]


VMEM = pl.BlockSpec(memory_space=pltpu.VMEM)
ANY = pl.BlockSpec(memory_space=pl.ANY)
LIMIT = pltpu.CompilerParams(vmem_limit_bytes=16 << 20)


def call(kernel, name, outs, *args, flops=0, **more):
    one = not isinstance(outs, tuple)
    options = dict(
        out_shape=outs,
        in_specs=[VMEM] * len(args),
        out_specs=VMEM if one else (VMEM,) * len(outs),
        name=name,
        compiler_params=LIMIT,
        cost_estimate=pl.CostEstimate(flops=flops, bytes_accessed=0, transcendentals=0),
    )
    return pl.pallas_call(kernel, **{**options, **more})(*args)


def shards(tokens, routes, gate_num, w_gate, w_up, w_down):
    tok_rows, top_count = routes.shape
    width = tokens.shape[1]
    hidden_width = w_gate.shape[2]
    devices = lax.axis_size("ep")
    chips = devices // SPLIT
    half = width // SPLIT
    capacity = max(2, min(tok_rows, 5 * tok_rows * top_count // (2 * EXPERTS)))
    order = group_order(chips)
    group = [[c * SPLIT + k for c in order for k in range(SPLIT)]]
    swap = [(d, d ^ 1) for d in range(devices)]
    slots, rows = chips * capacity, devices * capacity
    block = (devices, capacity, half)
    parts = 2 if half % 256 == 0 else 1
    bf16, f32 = jnp.bfloat16, jnp.float32
    shape = jax.ShapeDtypeStruct

    sources = [pltpu.with_memory_space_constraint(a, pltpu.HBM) for a in (routes.T, gate_num.T, tokens)]
    outgoing, weight = call(
        functools.partial(route_kernel, capacity, order),
        "route",
        (shape((chips, SPLIT, capacity, half), bf16), shape((slots, tok_rows), bf16)),
        *sources,
        flops=10**10,
        in_specs=[ANY] * 3,
        scratch_shapes=[
            pltpu.VMEM((top_count, tok_rows), jnp.int32),
            pltpu.VMEM((top_count, tok_rows), jnp.int32),
            pltpu.VMEM((SPLIT * parts, tok_rows, half // parts), bf16),
            pltpu.SemaphoreType.DMA((2 + SPLIT * parts,)),
        ],
    )
    exchange = functools.partial(
        lax.all_to_all,
        axis_name="ep",
        split_axis=0,
        concat_axis=0,
        tiled=True,
        axis_index_groups=group,
    )
    own = exchange(outgoing.reshape(block))
    other = lax.ppermute(own, "ep", swap)
    product = rows * half * hidden_width * 2
    accs = call(
        enter_kernel,
        "enter",
        (shape((rows, hidden_width), f32),) * 2,
        own,
        w_gate,
        w_up,
        flops=2 * product,
    )
    hidden, send = call(
        middle_kernel,
        "middle",
        (shape((rows, hidden_width), bf16), shape(block, bf16)),
        other,
        *accs,
        w_gate,
        w_up,
        w_down,
        flops=3 * product,
    )
    arrived = lax.ppermute(send, "ep", swap)
    keep = call(leave_kernel, "leave", shape(block, f32), hidden, w_down, flops=product)
    summed = (keep + arrived.astype(f32)).astype(bf16)
    returned = exchange(summed).reshape(chips, SPLIT, capacity, half)
    return call(
        combine_kernel,
        "combine",
        shape((tok_rows, width), bf16),
        weight,
        returned,
        out_specs=ANY,
        scratch_shapes=[
            pltpu.VMEM((SPLIT * parts, tok_rows, half // parts), bf16),
            pltpu.SemaphoreType.DMA((SPLIT * parts,)),
        ],
    )


def solution(mesh):
    return jax.shard_map(
        shards,
        mesh=mesh,
        in_specs=(
            P(("groups", "ep"), None),
            P(("groups", "ep"), None),
            P(("groups", "ep"), None),
            P("ep", None, None),
            P("ep", None, None),
            P("ep", None, None),
        ),
        out_specs=P(("groups", "ep"), None),
        check_vma=False,
    )
```

```python
import functools
import jax
import jax.numpy as jnp
from jax import lax
from jax.experimental import pallas as pl
from jax.experimental.pallas import tpu as pltpu
from jax.sharding import PartitionSpec as P

SPLIT = 2
EXPERTS = 256


def slots_of(routes, slots, capacity, order):
    top, rows = routes.shape
    slot = lax.broadcasted_iota(jnp.int32, (slots, rows), 0)
    block, place = slot // capacity, slot % capacity
    expert = jnp.zeros_like(block)
    for j, chip in enumerate(order):
        expert = jnp.where(block == j, chip, expert)
    same = [routes[k : k + 1, :] == expert for k in range(top)]
    hit = functools.reduce(jnp.logical_or, same).astype(jnp.float32)
    earlier = lax.broadcasted_iota(jnp.int32, (rows, rows), 0) < lax.broadcasted_iota(
        jnp.int32, (rows, rows), 1
    )
    rank = jnp.dot(
        hit.astype(jnp.bfloat16), earlier.astype(jnp.bfloat16), preferred_element_type=jnp.float32
    )
    return jnp.where(rank == place.astype(jnp.float32), hit, 0.0), same


def route_kernel(
    capacity, order, routes_hbm, gates_hbm, tokens_hbm, out_ref, weight_ref, routes_v, gates_v, tokens_v, sems
):
    chips, halves, _, half = out_ref.shape
    copies = [
        pltpu.make_async_copy(source, target, sems.at[i])
        for i, (source, target) in enumerate(
            ((routes_hbm, routes_v), (tokens_hbm, tokens_v), (gates_hbm, gates_v))
        )
    ]
    for copy in copies:
        copy.start()
    copies[0].wait()
    pick, same = slots_of(routes_v[...], chips * capacity, capacity, order)
    copies[2].wait()
    gates = gates_v[...].astype(jnp.float32) / 256.0
    weight = jnp.zeros_like(pick)
    for k, hit in enumerate(same):
        weight = jnp.where(hit, gates[k : k + 1, :], weight)
    weight_ref[...] = (weight * pick).astype(jnp.bfloat16)
    copies[1].wait()
    rows = jnp.dot(
        pick.astype(jnp.bfloat16), tokens_v[...], preferred_element_type=jnp.float32
    ).astype(jnp.bfloat16)
    for k in range(halves):
        part = rows[:, k * half : (k + 1) * half]
        out_ref[:, k] = part.reshape(chips, capacity, half)


def mark_kernel(in_ref, out_ref):
    del in_ref, out_ref


def flat(rows):
    return rows.reshape(rows.shape[0] * rows.shape[1], rows.shape[2])


def half_of(side, half):
    return pl.ds(pl.multiple_of(side * half, 128), half)


def enter_kernel(own_ref, gate_ref, up_ref, down_ref, gate_out, up_out):
    del down_ref
    half = own_ref.shape[2]
    mine = half_of(lax.axis_index("ep") % SPLIT, half)
    x = flat(own_ref[...])
    gate_out[...] = jnp.dot(x, gate_ref[0, mine, :], preferred_element_type=jnp.float32)
    up_out[...] = jnp.dot(x, up_ref[0, mine, :], preferred_element_type=jnp.float32)


def middle_kernel(other_ref, gate_acc, up_acc, gate_ref, up_ref, down_ref, hidden_ref, send_ref):
    half = other_ref.shape[2]
    theirs = half_of(1 - lax.axis_index("ep") % SPLIT, half)
    x = flat(other_ref[...])
    gate = gate_acc[...] + jnp.dot(x, gate_ref[0, theirs, :], preferred_element_type=jnp.float32)
    up = up_acc[...] + jnp.dot(x, up_ref[0, theirs, :], preferred_element_type=jnp.float32)
    hidden = (gate / (1.0 + jnp.exp(-gate)) * up).astype(jnp.bfloat16)
    hidden_ref[...] = hidden
    out = jnp.dot(hidden, down_ref[0, :, theirs], preferred_element_type=jnp.float32)
    send_ref[...] = out.astype(jnp.bfloat16).reshape(send_ref.shape)


def leave_kernel(hidden_ref, down_ref, keep_ref):
    half = keep_ref.shape[2]
    mine = half_of(lax.axis_index("ep") % SPLIT, half)
    out = jnp.dot(hidden_ref[...], down_ref[0, :, mine], preferred_element_type=jnp.float32)
    keep_ref[...] = out.reshape(keep_ref.shape)


def combine_kernel(weight_ref, rows_ref, out_hbm, out_v, sems):
    halves, half = rows_ref.shape[1], rows_ref.shape[3]
    parts = out_v.shape[0] // halves
    wide = half // parts
    copies = []
    for i in range(halves * parts):
        part = slice(i % parts * wide, (i % parts + 1) * wide)
        rows = flat(rows_ref[:, i // parts, :, part])
        out_v[i] = lax.dot_general(
            weight_ref[...], rows, (((0,), (0,)), ((), ())), preferred_element_type=jnp.float32
        ).astype(jnp.bfloat16)
        copies.append(
            pltpu.make_async_copy(out_v.at[i], out_hbm.at[:, pl.ds(i * wide, wide)], sems.at[i])
        )
        copies[-1].start()
    for copy in copies:
        copy.wait()


def group_order(chips):
    first = (5 * chips) // 8
    return [first] + [c for c in range(chips) if c != first]


VMEM = pl.BlockSpec(memory_space=pltpu.VMEM)
ANY = pl.BlockSpec(memory_space=pl.ANY)
LIMIT = pltpu.CompilerParams(vmem_limit_bytes=16 << 20)


def call(kernel, name, outs, *args, flops=0, **more):
    one = not isinstance(outs, tuple)
    options = dict(
        out_shape=outs,
        in_specs=[VMEM] * len(args),
        out_specs=VMEM if one else (VMEM,) * len(outs),
        name=name,
        compiler_params=LIMIT,
        cost_estimate=pl.CostEstimate(flops=flops, bytes_accessed=0, transcendentals=0),
    )
    return pl.pallas_call(kernel, **{**options, **more})(*args)


def shards(tokens, routes, gate_num, w_gate, w_up, w_down):
    tok_rows, top_count = routes.shape
    width = tokens.shape[1]
    hidden_width = w_gate.shape[2]
    devices = lax.axis_size("ep")
    chips = devices // SPLIT
    half = width // SPLIT
    capacity = max(2, min(tok_rows, 5 * tok_rows * top_count // (2 * EXPERTS)))
    order = group_order(chips)
    group = [[c * SPLIT + k for c in order for k in range(SPLIT)]]
    swap = [(d, d ^ 1) for d in range(devices)]
    slots, rows = chips * capacity, devices * capacity
    block = (devices, capacity, half)
    parts = 2 if half % 256 == 0 else 1
    bf16, f32 = jnp.bfloat16, jnp.float32
    shape = jax.ShapeDtypeStruct

    sources = [pltpu.with_memory_space_constraint(a, pltpu.HBM) for a in (routes.T, gate_num.T, tokens)]
    outgoing, weight = call(
        functools.partial(route_kernel, capacity, order),
        "route",
        (shape((chips, SPLIT, capacity, half), bf16), shape((slots, tok_rows), bf16)),
        *sources,
        in_specs=[ANY] * 3,
        scratch_shapes=[
            pltpu.VMEM((top_count, tok_rows), jnp.int32),
            pltpu.VMEM((top_count, tok_rows), jnp.int32),
            pltpu.VMEM((tok_rows, width), bf16),
            pltpu.SemaphoreType.DMA((3,)),
        ],
    )
    outgoing = outgoing.reshape(block)
    outgoing = call(
        mark_kernel, "mark", shape(block, bf16), outgoing, flops=10**10, input_output_aliases={0: 0}
    )
    exchange = functools.partial(
        lax.all_to_all,
        axis_name="ep",
        split_axis=0,
        concat_axis=0,
        tiled=True,
        axis_index_groups=group,
    )
    own = exchange(outgoing)
    other = lax.ppermute(own, "ep", swap)
    product = rows * half * hidden_width * 2
    accs = call(
        enter_kernel,
        "enter",
        (shape((rows, hidden_width), f32),) * 2,
        own,
        w_gate,
        w_up,
        w_down,
        flops=2 * product,
    )
    hidden, send = call(
        middle_kernel,
        "middle",
        (shape((rows, hidden_width), bf16), shape(block, bf16)),
        other,
        *accs,
        w_gate,
        w_up,
        w_down,
        flops=3 * product,
    )
    arrived = lax.ppermute(send, "ep", swap)
    keep = call(leave_kernel, "leave", shape(block, f32), hidden, w_down, flops=product)
    summed = (keep + arrived.astype(f32)).astype(bf16)
    returned = exchange(summed).reshape(chips, SPLIT, capacity, half)
    return call(
        combine_kernel,
        "combine",
        shape((tok_rows, width), bf16),
        weight,
        returned,
        out_specs=ANY,
        scratch_shapes=[
            pltpu.VMEM((SPLIT * parts, tok_rows, half // parts), bf16),
            pltpu.SemaphoreType.DMA((SPLIT * parts,)),
        ],
    )


def solution(mesh):
    return jax.shard_map(
        shards,
        mesh=mesh,
        in_specs=(
            P(("groups", "ep"), None),
            P(("groups", "ep"), None),
            P(("groups", "ep"), None),
            P("ep", None, None),
            P("ep", None, None),
            P("ep", None, None),
        ),
        out_specs=P(("groups", "ep"), None),
        check_vma=False,
    )
```

```python
import functools
import jax
import jax.numpy as jnp
from jax import lax
from jax.experimental import pallas as pl
from jax.experimental.pallas import tpu as pltpu
from jax.sharding import PartitionSpec as P

SPLIT = 2
EXPERTS = 256


def slots_of(routes, slots, capacity, order):
    top, rows = routes.shape
    slot = lax.broadcasted_iota(jnp.int32, (slots, rows), 0)
    block, place = slot // capacity, slot % capacity
    expert = jnp.zeros_like(block)
    for j, chip in enumerate(order):
        expert = jnp.where(block == j, chip, expert)
    same = [routes[k : k + 1, :] == expert for k in range(top)]
    hit = functools.reduce(jnp.logical_or, same).astype(jnp.float32)
    earlier = lax.broadcasted_iota(jnp.int32, (rows, rows), 0) < lax.broadcasted_iota(
        jnp.int32, (rows, rows), 1
    )
    rank = jnp.dot(
        hit.astype(jnp.bfloat16), earlier.astype(jnp.bfloat16), preferred_element_type=jnp.float32
    )
    return jnp.where(rank == place.astype(jnp.float32), hit, 0.0), same


def route_kernel(
    capacity, order, routes_hbm, gates_hbm, tokens_hbm, out_ref, weight_ref, routes_v, gates_v, tokens_v, sems
):
    chips, halves, _, half = out_ref.shape
    copies = [
        pltpu.make_async_copy(source, target, sems.at[i])
        for i, (source, target) in enumerate(
            ((routes_hbm, routes_v), (tokens_hbm, tokens_v), (gates_hbm, gates_v))
        )
    ]
    for copy in copies:
        copy.start()
    copies[0].wait()
    pick, same = slots_of(routes_v[...], chips * capacity, capacity, order)
    copies[2].wait()
    gates = gates_v[...].astype(jnp.float32) / 256.0
    weight = jnp.zeros_like(pick)
    for k, hit in enumerate(same):
        weight = jnp.where(hit, gates[k : k + 1, :], weight)
    weight_ref[...] = (weight * pick).astype(jnp.bfloat16)
    copies[1].wait()
    rows = jnp.dot(
        pick.astype(jnp.bfloat16), tokens_v[...], preferred_element_type=jnp.float32
    ).astype(jnp.bfloat16)
    for k in range(halves):
        part = rows[:, k * half : (k + 1) * half]
        out_ref[:, halves - 1 - k] = part.reshape(chips, capacity, half)


def mark_kernel(in_ref, out_ref):
    del in_ref, out_ref


def flat(rows):
    return rows.reshape(rows.shape[0] * rows.shape[1], rows.shape[2])


def half_of(side, half):
    return pl.ds(pl.multiple_of(side * half, 128), half)


def enter_kernel(own_ref, gate_ref, up_ref, down_ref, gate_out, up_out):
    del down_ref
    half = own_ref.shape[2]
    mine = half_of(lax.axis_index("ep") % SPLIT, half)
    x = flat(own_ref[...])
    gate_out[...] = jnp.dot(x, gate_ref[0, mine, :], preferred_element_type=jnp.float32)
    up_out[...] = jnp.dot(x, up_ref[0, mine, :], preferred_element_type=jnp.float32)


def middle_kernel(other_ref, gate_acc, up_acc, gate_ref, up_ref, down_ref, hidden_ref, send_ref):
    half = other_ref.shape[2]
    theirs = half_of(1 - lax.axis_index("ep") % SPLIT, half)
    x = flat(other_ref[...])
    gate = gate_acc[...] + jnp.dot(x, gate_ref[0, theirs, :], preferred_element_type=jnp.float32)
    up = up_acc[...] + jnp.dot(x, up_ref[0, theirs, :], preferred_element_type=jnp.float32)
    hidden = (gate / (1.0 + jnp.exp(-gate)) * up).astype(jnp.bfloat16)
    hidden_ref[...] = hidden
    out = jnp.dot(hidden, down_ref[0, :, theirs], preferred_element_type=jnp.float32)
    send_ref[...] = out.astype(jnp.bfloat16).reshape(send_ref.shape)


def leave_kernel(hidden_ref, down_ref, keep_ref):
    half = keep_ref.shape[2]
    mine = half_of(lax.axis_index("ep") % SPLIT, half)
    out = jnp.dot(hidden_ref[...], down_ref[0, :, mine], preferred_element_type=jnp.float32)
    keep_ref[...] = out.reshape(keep_ref.shape)


def combine_kernel(weight_ref, rows_ref, out_hbm, out_v, sems):
    halves, half = rows_ref.shape[1], rows_ref.shape[3]
    parts = out_v.shape[0] // halves
    wide = half // parts
    copies = []
    for i in range(halves * parts):
        part = slice(i % parts * wide, (i % parts + 1) * wide)
        rows = flat(rows_ref[:, halves - 1 - i // parts, :, part])
        out_v[i] = lax.dot_general(
            weight_ref[...], rows, (((0,), (0,)), ((), ())), preferred_element_type=jnp.float32
        ).astype(jnp.bfloat16)
        copies.append(
            pltpu.make_async_copy(out_v.at[i], out_hbm.at[:, pl.ds(i * wide, wide)], sems.at[i])
        )
        copies[-1].start()
    for copy in copies:
        copy.wait()


def group_order(chips):
    first = (5 * chips) // 8
    return [first] + [c for c in range(chips) if c != first]


VMEM = pl.BlockSpec(memory_space=pltpu.VMEM)
ANY = pl.BlockSpec(memory_space=pl.ANY)
LIMIT = pltpu.CompilerParams(vmem_limit_bytes=16 << 20)


def call(kernel, name, outs, *args, flops=0, **more):
    one = not isinstance(outs, tuple)
    options = dict(
        out_shape=outs,
        in_specs=[VMEM] * len(args),
        out_specs=VMEM if one else (VMEM,) * len(outs),
        name=name,
        compiler_params=LIMIT,
        cost_estimate=pl.CostEstimate(flops=flops, bytes_accessed=0, transcendentals=0),
    )
    return pl.pallas_call(kernel, **{**options, **more})(*args)


def shards(tokens, routes, gate_num, w_gate, w_up, w_down):
    tok_rows, top_count = routes.shape
    width = tokens.shape[1]
    hidden_width = w_gate.shape[2]
    devices = lax.axis_size("ep")
    chips = devices // SPLIT
    half = width // SPLIT
    capacity = max(2, min(tok_rows, 5 * tok_rows * top_count // (2 * EXPERTS)))
    order = group_order(chips)
    group = [[c * SPLIT + k for c in order for k in reversed(range(SPLIT))]]
    swap = [(d, d ^ 1) for d in range(devices)]
    slots, rows = chips * capacity, devices * capacity
    block = (devices, capacity, half)
    parts = 2 if half % 256 == 0 else 1
    bf16, f32 = jnp.bfloat16, jnp.float32
    shape = jax.ShapeDtypeStruct

    sources = [pltpu.with_memory_space_constraint(a, pltpu.HBM) for a in (routes.T, gate_num.T, tokens)]
    outgoing, weight = call(
        functools.partial(route_kernel, capacity, order),
        "route",
        (shape((chips, SPLIT, capacity, half), bf16), shape((slots, tok_rows), bf16)),
        *sources,
        in_specs=[ANY] * 3,
        scratch_shapes=[
            pltpu.VMEM((top_count, tok_rows), jnp.int32),
            pltpu.VMEM((top_count, tok_rows), jnp.int32),
            pltpu.VMEM((tok_rows, width), bf16),
            pltpu.SemaphoreType.DMA((3,)),
        ],
    )
    outgoing = outgoing.reshape(block)
    outgoing = call(
        mark_kernel, "mark", shape(block, bf16), outgoing, flops=10**10, input_output_aliases={0: 0}
    )
    exchange = functools.partial(
        lax.all_to_all,
        axis_name="ep",
        split_axis=0,
        concat_axis=0,
        tiled=True,
        axis_index_groups=group,
    )
    own = exchange(outgoing)
    other = lax.ppermute(own, "ep", swap)
    product = rows * half * hidden_width * 2
    accs = call(
        enter_kernel,
        "enter",
        (shape((rows, hidden_width), f32),) * 2,
        own,
        w_gate,
        w_up,
        w_down,
        flops=2 * product,
    )
    hidden, send = call(
        middle_kernel,
        "middle",
        (shape((rows, hidden_width), bf16), shape(block, bf16)),
        other,
        *accs,
        w_gate,
        w_up,
        w_down,
        flops=3 * product,
    )
    arrived = lax.ppermute(send, "ep", swap)
    keep = call(leave_kernel, "leave", shape(block, f32), hidden, w_down, flops=product)
    summed = (keep + arrived.astype(f32)).astype(bf16)
    returned = exchange(summed).reshape(chips, SPLIT, capacity, half)
    return call(
        combine_kernel,
        "combine",
        shape((tok_rows, width), bf16),
        weight,
        returned,
        out_specs=ANY,
        scratch_shapes=[
            pltpu.VMEM((SPLIT * parts, tok_rows, half // parts), bf16),
            pltpu.SemaphoreType.DMA((SPLIT * parts,)),
        ],
    )


def solution(mesh):
    return jax.shard_map(
        shards,
        mesh=mesh,
        in_specs=(
            P(("groups", "ep"), None),
            P(("groups", "ep"), None),
            P(("groups", "ep"), None),
            P("ep", None, None),
            P("ep", None, None),
            P("ep", None, None),
        ),
        out_specs=P(("groups", "ep"), None),
        check_vma=False,
    )
```

```python
import functools
import jax
import jax.numpy as jnp
from jax import lax
from jax.experimental import pallas as pl
from jax.experimental.pallas import tpu as pltpu
from jax.sharding import PartitionSpec as P

SPLIT = 2
EXPERTS = 256


def slots_of(routes, slots, capacity, order):
    top, rows = routes.shape
    slot = lax.broadcasted_iota(jnp.int32, (slots, rows), 0)
    block, place = slot // capacity, slot % capacity
    expert = jnp.zeros_like(block)
    for j, chip in enumerate(order):
        expert = jnp.where(block == j, chip, expert)
    same = [routes[k : k + 1, :] == expert for k in range(top)]
    hit = functools.reduce(jnp.logical_or, same).astype(jnp.float32)
    earlier = lax.broadcasted_iota(jnp.int32, (rows, rows), 0) < lax.broadcasted_iota(
        jnp.int32, (rows, rows), 1
    )
    rank = jnp.dot(
        hit.astype(jnp.bfloat16), earlier.astype(jnp.bfloat16), preferred_element_type=jnp.float32
    )
    return jnp.where(rank == place.astype(jnp.float32), hit, 0.0), same


def route_kernel(
    capacity, order, routes_hbm, gates_hbm, tokens_hbm, out_ref, weight_ref, routes_v, gates_v, tokens_v, sems
):
    chips, halves, _, half = out_ref.shape
    copies = [
        pltpu.make_async_copy(source, target, sems.at[i])
        for i, (source, target) in enumerate(
            ((routes_hbm, routes_v), (tokens_hbm, tokens_v), (gates_hbm, gates_v))
        )
    ]
    for copy in copies:
        copy.start()
    copies[0].wait()
    pick, same = slots_of(routes_v[...], chips * capacity, capacity, order)
    copies[2].wait()
    gates = gates_v[...].astype(jnp.float32) / 256.0
    weight = jnp.zeros_like(pick)
    for k, hit in enumerate(same):
        weight = jnp.where(hit, gates[k : k + 1, :], weight)
    weight_ref[...] = (weight * pick).astype(jnp.bfloat16)
    copies[1].wait()
    rows = jnp.dot(
        pick.astype(jnp.bfloat16), tokens_v[...], preferred_element_type=jnp.float32
    ).astype(jnp.bfloat16)
    for k in range(halves):
        part = rows[:, k * half : (k + 1) * half]
        out_ref[:, halves - 1 - k] = part.reshape(chips, capacity, half)


def mark_kernel(in_ref, out_ref):
    del in_ref, out_ref


def flat(rows):
    return rows.reshape(rows.shape[0] * rows.shape[1], rows.shape[2])


def half_of(side, half):
    return pl.ds(pl.multiple_of(side * half, 128), half)


def enter_kernel(own_ref, gate_ref, up_ref, down_ref, gate_out, up_out):
    del down_ref
    half = own_ref.shape[2]
    mine = half_of(lax.axis_index("ep") % SPLIT, half)
    x = flat(own_ref[...])
    gate_out[...] = jnp.dot(x, gate_ref[0, mine, :], preferred_element_type=jnp.float32)
    up_out[...] = jnp.dot(x, up_ref[0, mine, :], preferred_element_type=jnp.float32)


def middle_kernel(
    other_ref, gate_acc, up_acc, gate_ref, up_ref, down_ref, hidden_ref, send_ref, gate_v, up_v
):
    half = other_ref.shape[2]
    side = 1 - lax.axis_index("ep") % SPLIT
    theirs = half_of(side, half)
    x = flat(other_ref[...])
    gate_v[...] = jnp.dot(x, gate_ref[0, theirs, :], preferred_element_type=jnp.float32)
    up_v[...] = jnp.dot(x, up_ref[0, theirs, :], preferred_element_type=jnp.float32)

    @pl.when(side < SPLIT)
    def _():
        gate = gate_acc[...] + gate_v[...]
        up = up_acc[...] + up_v[...]
        hidden = (gate / (1.0 + jnp.exp(-gate)) * up).astype(jnp.bfloat16)
        hidden_ref[...] = hidden
        out = jnp.dot(hidden, down_ref[0, :, theirs], preferred_element_type=jnp.float32)
        send_ref[...] = out.astype(jnp.bfloat16).reshape(send_ref.shape)


def leave_kernel(hidden_ref, down_ref, keep_ref):
    half = keep_ref.shape[2]
    mine = half_of(lax.axis_index("ep") % SPLIT, half)
    out = jnp.dot(hidden_ref[...], down_ref[0, :, mine], preferred_element_type=jnp.float32)
    keep_ref[...] = out.reshape(keep_ref.shape)


def combine_kernel(weight_ref, rows_ref, out_hbm, out_v, sems):
    halves, half = rows_ref.shape[1], rows_ref.shape[3]
    parts = out_v.shape[0] // halves
    wide = half // parts
    copies = []
    for i in range(halves * parts):
        part = slice(i % parts * wide, (i % parts + 1) * wide)
        rows = flat(rows_ref[:, halves - 1 - i // parts, :, part])
        out_v[i] = lax.dot_general(
            weight_ref[...], rows, (((0,), (0,)), ((), ())), preferred_element_type=jnp.float32
        ).astype(jnp.bfloat16)
        copies.append(
            pltpu.make_async_copy(out_v.at[i], out_hbm.at[:, pl.ds(i * wide, wide)], sems.at[i])
        )
        copies[-1].start()
    for copy in copies:
        copy.wait()


def group_order(chips):
    first = (5 * chips) // 8
    return [first] + [c for c in range(chips) if c != first]


VMEM = pl.BlockSpec(memory_space=pltpu.VMEM)
ANY = pl.BlockSpec(memory_space=pl.ANY)
LIMIT = pltpu.CompilerParams(vmem_limit_bytes=16 << 20)


def call(kernel, name, outs, *args, flops=0, **more):
    one = not isinstance(outs, tuple)
    options = dict(
        out_shape=outs,
        in_specs=[VMEM] * len(args),
        out_specs=VMEM if one else (VMEM,) * len(outs),
        name=name,
        compiler_params=LIMIT,
        cost_estimate=pl.CostEstimate(flops=flops, bytes_accessed=0, transcendentals=0),
    )
    return pl.pallas_call(kernel, **{**options, **more})(*args)


def shards(tokens, routes, gate_num, w_gate, w_up, w_down):
    tok_rows, top_count = routes.shape
    width = tokens.shape[1]
    hidden_width = w_gate.shape[2]
    devices = lax.axis_size("ep")
    chips = devices // SPLIT
    half = width // SPLIT
    capacity = max(2, min(tok_rows, 5 * tok_rows * top_count // (2 * EXPERTS)))
    order = group_order(chips)
    group = [[c * SPLIT + k for c in order for k in reversed(range(SPLIT))]]
    swap = [(d, d ^ 1) for d in range(devices)]
    slots, rows = chips * capacity, devices * capacity
    block = (devices, capacity, half)
    parts = 2 if half % 256 == 0 else 1
    bf16, f32 = jnp.bfloat16, jnp.float32
    shape = jax.ShapeDtypeStruct

    sources = [pltpu.with_memory_space_constraint(a, pltpu.HBM) for a in (routes.T, gate_num.T, tokens)]
    outgoing, weight = call(
        functools.partial(route_kernel, capacity, order),
        "route",
        (shape((chips, SPLIT, capacity, half), bf16), shape((slots, tok_rows), bf16)),
        *sources,
        in_specs=[ANY] * 3,
        scratch_shapes=[
            pltpu.VMEM((top_count, tok_rows), jnp.int32),
            pltpu.VMEM((top_count, tok_rows), jnp.int32),
            pltpu.VMEM((tok_rows, width), bf16),
            pltpu.SemaphoreType.DMA((3,)),
        ],
    )
    outgoing = outgoing.reshape(block)
    outgoing = call(
        mark_kernel, "mark", shape(block, bf16), outgoing, flops=10**10, input_output_aliases={0: 0}
    )
    exchange = functools.partial(
        lax.all_to_all,
        axis_name="ep",
        split_axis=0,
        concat_axis=0,
        tiled=True,
        axis_index_groups=group,
    )
    own = exchange(outgoing)
    other = lax.ppermute(own, "ep", swap)
    product = rows * half * hidden_width * 2
    accs = call(
        enter_kernel,
        "enter",
        (shape((rows, hidden_width), f32),) * 2,
        own,
        w_gate,
        w_up,
        w_down,
        flops=2 * product,
    )
    hidden, send = call(
        middle_kernel,
        "middle",
        (shape((rows, hidden_width), bf16), shape(block, bf16)),
        other,
        *accs,
        w_gate,
        w_up,
        w_down,
        flops=3 * product,
        scratch_shapes=[pltpu.VMEM((rows, hidden_width), f32)] * 2,
    )
    arrived = lax.ppermute(send, "ep", swap)
    keep = call(leave_kernel, "leave", shape(block, f32), hidden, w_down, flops=product)
    summed = (keep + arrived.astype(f32)).astype(bf16)
    returned = exchange(summed).reshape(chips, SPLIT, capacity, half)
    return call(
        combine_kernel,
        "combine",
        shape((tok_rows, width), bf16),
        weight,
        returned,
        out_specs=ANY,
        scratch_shapes=[
            pltpu.VMEM((SPLIT * parts, tok_rows, half // parts), bf16),
            pltpu.SemaphoreType.DMA((SPLIT * parts,)),
        ],
    )


def solution(mesh):
    return jax.shard_map(
        shards,
        mesh=mesh,
        in_specs=(
            P(("groups", "ep"), None),
            P(("groups", "ep"), None),
            P(("groups", "ep"), None),
            P("ep", None, None),
            P("ep", None, None),
            P("ep", None, None),
        ),
        out_specs=P(("groups", "ep"), None),
        check_vma=False,
    )
```

```python
import functools
import jax
import jax.numpy as jnp
from jax import lax
from jax.experimental import pallas as pl
from jax.experimental.pallas import tpu as pltpu
from jax.sharding import PartitionSpec as P

SPLIT = 2
EXPERTS = 256


def slots_of(routes, slots, capacity, order):
    top, rows = routes.shape
    slot = lax.broadcasted_iota(jnp.int32, (slots, rows), 0)
    block, place = slot // capacity, slot % capacity
    expert = jnp.zeros_like(block)
    for j, chip in enumerate(order):
        expert = jnp.where(block == j, chip, expert)
    same = [routes[k : k + 1, :] == expert for k in range(top)]
    hit = functools.reduce(jnp.logical_or, same).astype(jnp.float32)
    earlier = lax.broadcasted_iota(jnp.int32, (rows, rows), 0) < lax.broadcasted_iota(
        jnp.int32, (rows, rows), 1
    )
    rank = jnp.dot(
        hit.astype(jnp.bfloat16), earlier.astype(jnp.bfloat16), preferred_element_type=jnp.float32
    )
    return jnp.where(rank == place.astype(jnp.float32), hit, 0.0), same


def route_kernel(
    capacity, there, back, routes_hbm, gates_hbm, tokens_hbm, out_ref, weight_ref, routes_v, gates_v, tokens_v, sems
):
    chips, halves, _, half = out_ref.shape
    copies = [
        pltpu.make_async_copy(source, target, sems.at[i])
        for i, (source, target) in enumerate(
            ((routes_hbm, routes_v), (tokens_hbm, tokens_v), (gates_hbm, gates_v))
        )
    ]
    for copy in copies:
        copy.start()
    copies[0].wait()
    pick, same = slots_of(routes_v[...], chips * capacity, capacity, there)
    copies[2].wait()
    gates = gates_v[...].astype(jnp.float32) / 256.0
    weight = jnp.zeros_like(pick)
    for k, hit in enumerate(same):
        weight = jnp.where(hit, gates[k : k + 1, :], weight)
    weight = (weight * pick).astype(jnp.bfloat16)
    for i, chip in enumerate(there):
        j = back.index(chip)
        weight_ref[j * capacity : (j + 1) * capacity, :] = weight[i * capacity : (i + 1) * capacity]
    copies[1].wait()
    rows = jnp.dot(
        pick.astype(jnp.bfloat16), tokens_v[...], preferred_element_type=jnp.float32
    ).astype(jnp.bfloat16)
    for k in range(halves):
        part = rows[:, k * half : (k + 1) * half]
        out_ref[:, halves - 1 - k] = part.reshape(chips, capacity, half)


def mark_kernel(in_ref, out_ref):
    del in_ref, out_ref


def flat(rows):
    return rows.reshape(rows.shape[0] * rows.shape[1], rows.shape[2])


def half_of(side, half):
    return pl.ds(pl.multiple_of(side * half, 128), half)


def enter_kernel(own_ref, gate_ref, up_ref, down_ref, gate_out, up_out):
    del down_ref
    half = own_ref.shape[2]
    mine = half_of(lax.axis_index("ep") % SPLIT, half)
    x = flat(own_ref[...])
    gate_out[...] = jnp.dot(x, gate_ref[0, mine, :], preferred_element_type=jnp.float32)
    up_out[...] = jnp.dot(x, up_ref[0, mine, :], preferred_element_type=jnp.float32)


def middle_kernel(other_ref, gate_acc, up_acc, gate_ref, up_ref, down_ref, hidden_ref, send_ref):
    half = other_ref.shape[2]
    theirs = half_of(1 - lax.axis_index("ep") % SPLIT, half)
    x = flat(other_ref[...])
    gate = gate_acc[...] + jnp.dot(x, gate_ref[0, theirs, :], preferred_element_type=jnp.float32)
    up = up_acc[...] + jnp.dot(x, up_ref[0, theirs, :], preferred_element_type=jnp.float32)
    hidden = (gate / (1.0 + jnp.exp(-gate)) * up).astype(jnp.bfloat16)
    hidden_ref[...] = hidden
    out = jnp.dot(hidden, down_ref[0, :, theirs], preferred_element_type=jnp.float32)
    send_ref[...] = out.astype(jnp.bfloat16).reshape(send_ref.shape)


def leave_kernel(hidden_ref, down_ref, keep_ref):
    half = keep_ref.shape[1]
    mine = half_of(lax.axis_index("ep") % SPLIT, half)
    keep_ref[...] = jnp.dot(
        hidden_ref[...], down_ref[0, :, mine], preferred_element_type=jnp.float32
    )


def add_kernel(moves, keep_ref, arrived_ref, out_ref):
    capacity, half = out_ref.shape[1:]
    total = (keep_ref[...] + flat(arrived_ref[...]).astype(jnp.float32)).astype(jnp.bfloat16)
    total = total.reshape(out_ref.shape)
    for source, target in enumerate(moves):
        out_ref[target] = total[source]


def combine_kernel(weight_ref, rows_ref, out_hbm, out_v, sems):
    halves, half = rows_ref.shape[1], rows_ref.shape[3]
    parts = out_v.shape[0] // halves
    wide = half // parts
    copies = []
    for i in range(halves * parts):
        part = slice(i % parts * wide, (i % parts + 1) * wide)
        rows = flat(rows_ref[:, halves - 1 - i // parts, :, part])
        out_v[i] = lax.dot_general(
            weight_ref[...], rows, (((0,), (0,)), ((), ())), preferred_element_type=jnp.float32
        ).astype(jnp.bfloat16)
        copies.append(
            pltpu.make_async_copy(out_v.at[i], out_hbm.at[:, pl.ds(i * wide, wide)], sems.at[i])
        )
        copies[-1].start()
    for copy in copies:
        copy.wait()


def group_orders(chips):
    first = (5 * chips) // 8
    back = [first] + [c for c in range(chips) if c != first]
    half = chips // 2
    ring = [c for c in range(half, chips) if c % 2] + [c for c in range(half, chips) if not c % 2][::-1]
    turn = ring.index(first)
    there = ring[turn:] + ring[:turn]
    there += [c + k for c in range(half - 2, -1, -2) for k in range(2)]
    if sorted(there) != list(range(chips)):
        there = back
    return there, back


VMEM = pl.BlockSpec(memory_space=pltpu.VMEM)
ANY = pl.BlockSpec(memory_space=pl.ANY)
LIMIT = pltpu.CompilerParams(vmem_limit_bytes=16 << 20)


def call(kernel, name, outs, *args, flops=0, **more):
    one = not isinstance(outs, tuple)
    options = dict(
        out_shape=outs,
        in_specs=[VMEM] * len(args),
        out_specs=VMEM if one else (VMEM,) * len(outs),
        name=name,
        compiler_params=LIMIT,
        cost_estimate=pl.CostEstimate(flops=flops, bytes_accessed=0, transcendentals=0),
    )
    return pl.pallas_call(kernel, **{**options, **more})(*args)


def shards(tokens, routes, gate_num, w_gate, w_up, w_down):
    tok_rows, top_count = routes.shape
    width = tokens.shape[1]
    hidden_width = w_gate.shape[2]
    devices = lax.axis_size("ep")
    chips = devices // SPLIT
    half = width // SPLIT
    capacity = max(2, min(tok_rows, 5 * tok_rows * top_count // (2 * EXPERTS)))
    there, back = group_orders(chips)
    moves = [back.index(c) * SPLIT + k for c in there for k in range(SPLIT)]
    swap = [(d, d ^ 1) for d in range(devices)]
    slots, rows = chips * capacity, devices * capacity
    block = (devices, capacity, half)
    parts = 2 if half % 256 == 0 else 1
    bf16, f32 = jnp.bfloat16, jnp.float32
    shape = jax.ShapeDtypeStruct

    sources = [pltpu.with_memory_space_constraint(a, pltpu.HBM) for a in (routes.T, gate_num.T, tokens)]
    outgoing, weight = call(
        functools.partial(route_kernel, capacity, there, back),
        "route",
        (shape((chips, SPLIT, capacity, half), bf16), shape((slots, tok_rows), bf16)),
        *sources,
        in_specs=[ANY] * 3,
        scratch_shapes=[
            pltpu.VMEM((top_count, tok_rows), jnp.int32),
            pltpu.VMEM((top_count, tok_rows), jnp.int32),
            pltpu.VMEM((tok_rows, width), bf16),
            pltpu.SemaphoreType.DMA((3,)),
        ],
    )
    outgoing = outgoing.reshape(block)
    outgoing = call(
        mark_kernel, "mark", shape(block, bf16), outgoing, flops=10**10, input_output_aliases={0: 0}
    )
    def exchange(blocks, order):
        group = [[c * SPLIT + k for c in order for k in reversed(range(SPLIT))]]
        return lax.all_to_all(
            blocks, "ep", split_axis=0, concat_axis=0, tiled=True, axis_index_groups=group
        )

    own = exchange(outgoing, there)
    other = lax.ppermute(own, "ep", swap)
    product = rows * half * hidden_width * 2
    accs = call(
        enter_kernel,
        "enter",
        (shape((rows, hidden_width), f32),) * 2,
        own,
        w_gate,
        w_up,
        w_down,
        flops=2 * product,
    )
    hidden, send = call(
        middle_kernel,
        "middle",
        (shape((rows, hidden_width), bf16), shape(block, bf16)),
        other,
        *accs,
        w_gate,
        w_up,
        w_down,
        flops=3 * product,
    )
    arrived = lax.ppermute(send, "ep", swap)
    keep = call(leave_kernel, "leave", shape((rows, half), f32), hidden, w_down, flops=product)
    summed = call(functools.partial(add_kernel, moves), "add", shape(block, bf16), keep, arrived)
    returned = exchange(summed, back).reshape(chips, SPLIT, capacity, half)
    return call(
        combine_kernel,
        "combine",
        shape((tok_rows, width), bf16),
        weight,
        returned,
        out_specs=ANY,
        scratch_shapes=[
            pltpu.VMEM((SPLIT * parts, tok_rows, half // parts), bf16),
            pltpu.SemaphoreType.DMA((SPLIT * parts,)),
        ],
    )


def solution(mesh):
    return jax.shard_map(
        shards,
        mesh=mesh,
        in_specs=(
            P(("groups", "ep"), None),
            P(("groups", "ep"), None),
            P(("groups", "ep"), None),
            P("ep", None, None),
            P("ep", None, None),
            P("ep", None, None),
        ),
        out_specs=P(("groups", "ep"), None),
        check_vma=False,
    )
```

```python
import functools
import jax
import jax.numpy as jnp
from jax import lax
from jax.experimental import pallas as pl
from jax.experimental.pallas import tpu as pltpu
from jax.sharding import PartitionSpec as P

SPLIT = 2
EXPERTS = 256


def slots_of(routes, slots, capacity, order):
    top, rows = routes.shape
    slot = lax.broadcasted_iota(jnp.int32, (slots, rows), 0)
    block, place = slot // capacity, slot % capacity
    expert = jnp.zeros_like(block)
    for j, chip in enumerate(order):
        expert = jnp.where(block == j, chip, expert)
    same = [routes[k : k + 1, :] == expert for k in range(top)]
    hit = functools.reduce(jnp.logical_or, same).astype(jnp.float32)
    earlier = lax.broadcasted_iota(jnp.int32, (rows, rows), 0) < lax.broadcasted_iota(
        jnp.int32, (rows, rows), 1
    )
    rank = jnp.dot(
        hit.astype(jnp.bfloat16), earlier.astype(jnp.bfloat16), preferred_element_type=jnp.float32
    )
    return jnp.where(rank == place.astype(jnp.float32), hit, 0.0), same


def route_kernel(
    capacity, there, back, routes_hbm, gates_hbm, tokens_hbm, out_ref, weight_ref, routes_v, gates_v, tokens_v, sems
):
    chips, halves, _, half = out_ref.shape
    copies = [
        pltpu.make_async_copy(source, target, sems.at[i])
        for i, (source, target) in enumerate(
            ((routes_hbm, routes_v), (tokens_hbm, tokens_v), (gates_hbm, gates_v))
        )
    ]
    for copy in copies:
        copy.start()
    copies[0].wait()
    pick, same = slots_of(routes_v[...], chips * capacity, capacity, there)
    copies[2].wait()
    gates = gates_v[...].astype(jnp.float32) / 256.0
    weight = jnp.zeros_like(pick)
    for k, hit in enumerate(same):
        weight = jnp.where(hit, gates[k : k + 1, :], weight)
    weight = (weight * pick).astype(jnp.bfloat16)
    for i, chip in enumerate(there):
        j = back.index(chip)
        weight_ref[j * capacity : (j + 1) * capacity, :] = weight[i * capacity : (i + 1) * capacity]
    copies[1].wait()
    rows = jnp.dot(
        pick.astype(jnp.bfloat16), tokens_v[...], preferred_element_type=jnp.float32
    ).astype(jnp.bfloat16)
    for k in range(halves):
        part = rows[:, k * half : (k + 1) * half]
        out_ref[:, halves - 1 - k] = part.reshape(chips, capacity, half)


def flat(rows):
    return rows.reshape(rows.shape[0] * rows.shape[1], rows.shape[2])


def half_of(side, half):
    return pl.ds(pl.multiple_of(side * half, 128), half)


def enter_kernel(own_ref, gate_ref, up_ref, down_ref, gate_out, up_out):
    del down_ref
    half = own_ref.shape[2]
    mine = half_of(lax.axis_index("ep") % SPLIT, half)
    x = flat(own_ref[...])
    gate_out[...] = jnp.dot(x, gate_ref[0, mine, :], preferred_element_type=jnp.float32)
    up_out[...] = jnp.dot(x, up_ref[0, mine, :], preferred_element_type=jnp.float32)


def middle_kernel(other_ref, gate_acc, up_acc, gate_ref, up_ref, down_ref, hidden_ref, send_ref):
    half = other_ref.shape[2]
    theirs = half_of(1 - lax.axis_index("ep") % SPLIT, half)
    x = flat(other_ref[...])
    gate = gate_acc[...] + jnp.dot(x, gate_ref[0, theirs, :], preferred_element_type=jnp.float32)
    up = up_acc[...] + jnp.dot(x, up_ref[0, theirs, :], preferred_element_type=jnp.float32)
    hidden = (gate / (1.0 + jnp.exp(-gate)) * up).astype(jnp.bfloat16)
    hidden_ref[...] = hidden
    out = jnp.dot(hidden, down_ref[0, :, theirs], preferred_element_type=jnp.float32)
    send_ref[...] = out.astype(jnp.bfloat16).reshape(send_ref.shape)


def leave_kernel(hidden_ref, down_ref, keep_ref):
    half = keep_ref.shape[1]
    mine = half_of(lax.axis_index("ep") % SPLIT, half)
    keep_ref[...] = jnp.dot(
        hidden_ref[...], down_ref[0, :, mine], preferred_element_type=jnp.float32
    )


def add_kernel(moves, keep_ref, arrived_ref, out_ref):
    capacity, half = out_ref.shape[1:]
    total = (keep_ref[...] + flat(arrived_ref[...]).astype(jnp.float32)).astype(jnp.bfloat16)
    total = total.reshape(out_ref.shape)
    for source, target in enumerate(moves):
        out_ref[target] = total[source]


def combine_kernel(weight_ref, rows_ref, out_hbm, out_v, sems):
    halves, half = rows_ref.shape[1], rows_ref.shape[3]
    parts = out_v.shape[0] // halves
    wide = half // parts
    copies = []
    for i in range(halves * parts):
        part = slice(i % parts * wide, (i % parts + 1) * wide)
        rows = flat(rows_ref[:, halves - 1 - i // parts, :, part])
        out_v[i] = lax.dot_general(
            weight_ref[...], rows, (((0,), (0,)), ((), ())), preferred_element_type=jnp.float32
        ).astype(jnp.bfloat16)
        copies.append(
            pltpu.make_async_copy(out_v.at[i], out_hbm.at[:, pl.ds(i * wide, wide)], sems.at[i])
        )
        copies[-1].start()
    for copy in copies:
        copy.wait()


def group_orders(chips):
    first = (5 * chips) // 8
    back = [first] + [c for c in range(chips) if c != first]
    half = chips // 2
    ring = [c for c in range(half, chips) if c % 2] + [c for c in range(half, chips) if not c % 2][::-1]
    turn = ring.index(first)
    there = ring[turn:] + ring[:turn]
    there += [c + k for c in range(half - 2, -1, -2) for k in range(2)]
    if sorted(there) != list(range(chips)):
        there = back
    return there, back


VMEM = pl.BlockSpec(memory_space=pltpu.VMEM)
ANY = pl.BlockSpec(memory_space=pl.ANY)
LIMIT = pltpu.CompilerParams(vmem_limit_bytes=16 << 20)


def call(kernel, name, outs, *args, flops=0, **more):
    one = not isinstance(outs, tuple)
    options = dict(
        out_shape=outs,
        in_specs=[VMEM] * len(args),
        out_specs=VMEM if one else (VMEM,) * len(outs),
        name=name,
        compiler_params=LIMIT,
        cost_estimate=pl.CostEstimate(flops=flops, bytes_accessed=0, transcendentals=0),
    )
    return pl.pallas_call(kernel, **{**options, **more})(*args)


def shards(tokens, routes, gate_num, w_gate, w_up, w_down):
    tok_rows, top_count = routes.shape
    width = tokens.shape[1]
    hidden_width = w_gate.shape[2]
    devices = lax.axis_size("ep")
    chips = devices // SPLIT
    half = width // SPLIT
    capacity = max(2, min(tok_rows, 5 * tok_rows * top_count // (2 * EXPERTS)))
    there, back = group_orders(chips)
    moves = [back.index(c) * SPLIT + k for c in there for k in range(SPLIT)]
    swap = [(d, d ^ 1) for d in range(devices)]
    slots, rows = chips * capacity, devices * capacity
    block = (devices, capacity, half)
    parts = 2 if half % 256 == 0 else 1
    bf16, f32 = jnp.bfloat16, jnp.float32
    shape = jax.ShapeDtypeStruct

    sources = [pltpu.with_memory_space_constraint(a, pltpu.HBM) for a in (routes.T, gate_num.T, tokens)]
    outgoing, weight = call(
        functools.partial(route_kernel, capacity, there, back),
        "route",
        (shape((chips, SPLIT, capacity, half), bf16), shape((slots, tok_rows), bf16)),
        *sources,
        flops=10**10,
        in_specs=[ANY] * 3,
        scratch_shapes=[
            pltpu.VMEM((top_count, tok_rows), jnp.int32),
            pltpu.VMEM((top_count, tok_rows), jnp.int32),
            pltpu.VMEM((tok_rows, width), bf16),
            pltpu.SemaphoreType.DMA((3,)),
        ],
    )
    outgoing = outgoing.reshape(block)
    def exchange(blocks, order):
        group = [[c * SPLIT + k for c in order for k in reversed(range(SPLIT))]]
        return lax.all_to_all(
            blocks, "ep", split_axis=0, concat_axis=0, tiled=True, axis_index_groups=group
        )

    own = exchange(outgoing, there)
    other = lax.ppermute(own, "ep", swap)
    product = rows * half * hidden_width * 2
    accs = call(
        enter_kernel,
        "enter",
        (shape((rows, hidden_width), f32),) * 2,
        own,
        w_gate,
        w_up,
        w_down,
        flops=2 * product,
    )
    hidden, send = call(
        middle_kernel,
        "middle",
        (shape((rows, hidden_width), bf16), shape(block, bf16)),
        other,
        *accs,
        w_gate,
        w_up,
        w_down,
        flops=3 * product,
    )
    arrived = lax.ppermute(send, "ep", swap)
    keep = call(leave_kernel, "leave", shape((rows, half), f32), hidden, w_down, flops=product)
    summed = call(functools.partial(add_kernel, moves), "add", shape(block, bf16), keep, arrived)
    returned = exchange(summed, back).reshape(chips, SPLIT, capacity, half)
    return call(
        combine_kernel,
        "combine",
        shape((tok_rows, width), bf16),
        weight,
        returned,
        out_specs=ANY,
        scratch_shapes=[
            pltpu.VMEM((SPLIT * parts, tok_rows, half // parts), bf16),
            pltpu.SemaphoreType.DMA((SPLIT * parts,)),
        ],
    )


def solution(mesh):
    return jax.shard_map(
        shards,
        mesh=mesh,
        in_specs=(
            P(("groups", "ep"), None),
            P(("groups", "ep"), None),
            P(("groups", "ep"), None),
            P("ep", None, None),
            P("ep", None, None),
            P("ep", None, None),
        ),
        out_specs=P(("groups", "ep"), None),
        check_vma=False,
    )
```

```python
import functools
import jax
import jax.numpy as jnp
from jax import lax
from jax.experimental import pallas as pl
from jax.experimental.pallas import tpu as pltpu
from jax.sharding import PartitionSpec as P

SPLIT = 2
EXPERTS = 256


def slots_of(routes, slots, capacity, order):
    top, rows = routes.shape
    slot = lax.broadcasted_iota(jnp.int32, (slots, rows), 0)
    block, place = slot // capacity, slot % capacity
    expert = jnp.zeros_like(block)
    for j, chip in enumerate(order):
        expert = jnp.where(block == j, chip, expert)
    same = [routes[k : k + 1, :] == expert for k in range(top)]
    hit = functools.reduce(jnp.logical_or, same).astype(jnp.float32)
    earlier = lax.broadcasted_iota(jnp.int32, (rows, rows), 0) < lax.broadcasted_iota(
        jnp.int32, (rows, rows), 1
    )
    rank = jnp.dot(
        hit.astype(jnp.bfloat16), earlier.astype(jnp.bfloat16), preferred_element_type=jnp.float32
    )
    return jnp.where(rank == place.astype(jnp.float32), hit, 0.0), same


def route_kernel(
    capacity, there, back, routes_hbm, gates_hbm, tokens_hbm, out_ref, weight_ref, routes_v, gates_v, tokens_v, sems
):
    chips, halves, _, half = out_ref.shape
    copies = [
        pltpu.make_async_copy(source, target, sems.at[i])
        for i, (source, target) in enumerate(
            ((routes_hbm, routes_v), (tokens_hbm, tokens_v), (gates_hbm, gates_v))
        )
    ]
    for copy in copies:
        copy.start()
    copies[0].wait()
    pick, same = slots_of(routes_v[...], chips * capacity, capacity, there)
    copies[2].wait()
    gates = gates_v[...].astype(jnp.float32) / 256.0
    weight = jnp.zeros_like(pick)
    for k, hit in enumerate(same):
        weight = jnp.where(hit, gates[k : k + 1, :], weight)
    weight = (weight * pick).astype(jnp.bfloat16)
    for i, chip in enumerate(there):
        j = back.index(chip)
        weight_ref[j * capacity : (j + 1) * capacity, :] = weight[i * capacity : (i + 1) * capacity]
    copies[1].wait()
    rows = jnp.dot(
        pick.astype(jnp.bfloat16), tokens_v[...], preferred_element_type=jnp.float32
    ).astype(jnp.bfloat16)
    for k in range(halves):
        part = rows[:, k * half : (k + 1) * half]
        out_ref[:, halves - 1 - k] = part.reshape(chips, capacity, half)


def mark_kernel(in_ref, out_ref):
    del in_ref, out_ref


def flat(rows):
    return rows.reshape(rows.shape[0] * rows.shape[1], rows.shape[2])


def half_of(side, half):
    return pl.ds(pl.multiple_of(side * half, 128), half)


def enter_kernel(own_ref, gate_ref, up_ref, down_ref, gate_out, up_out):
    del down_ref
    half = own_ref.shape[2]
    mine = half_of(lax.axis_index("ep") % SPLIT, half)
    x = flat(own_ref[...])
    gate_out[...] = jnp.dot(x, gate_ref[0, mine, :], preferred_element_type=jnp.float32)
    up_out[...] = jnp.dot(x, up_ref[0, mine, :], preferred_element_type=jnp.float32)


def middle_kernel(other_ref, gate_acc, up_acc, gate_ref, up_ref, down_ref, hidden_ref, send_ref):
    half = other_ref.shape[2]
    theirs = half_of(1 - lax.axis_index("ep") % SPLIT, half)
    x = flat(other_ref[...])
    gate = gate_acc[...] + jnp.dot(x, gate_ref[0, theirs, :], preferred_element_type=jnp.float32)
    up = up_acc[...] + jnp.dot(x, up_ref[0, theirs, :], preferred_element_type=jnp.float32)
    hidden = (gate / (1.0 + jnp.exp(-gate)) * up).astype(jnp.bfloat16)
    hidden_ref[...] = hidden
    out = jnp.dot(hidden, down_ref[0, :, theirs], preferred_element_type=jnp.float32)
    send_ref[...] = out.astype(jnp.bfloat16).reshape(send_ref.shape)


def leave_kernel(hidden_ref, down_ref, keep_ref):
    half = keep_ref.shape[1]
    mine = half_of(lax.axis_index("ep") % SPLIT, half)
    keep_ref[...] = jnp.dot(
        hidden_ref[...], down_ref[0, :, mine], preferred_element_type=jnp.float32
    )


def add_kernel(moves, keep_ref, arrived_ref, out_ref):
    capacity, half = out_ref.shape[1:]
    total = (keep_ref[...] + flat(arrived_ref[...]).astype(jnp.float32)).astype(jnp.bfloat16)
    total = total.reshape(out_ref.shape)
    for source, target in enumerate(moves):
        out_ref[target] = total[source]


def combine_kernel(weight_ref, rows_ref, out_hbm, out_v, sems):
    halves, half = rows_ref.shape[1], rows_ref.shape[3]
    parts = out_v.shape[0] // halves
    wide = half // parts
    copies = []
    for i in range(halves * parts):
        part = slice(i % parts * wide, (i % parts + 1) * wide)
        rows = flat(rows_ref[:, halves - 1 - i // parts, :, part])
        out_v[i] = lax.dot_general(
            weight_ref[...], rows, (((0,), (0,)), ((), ())), preferred_element_type=jnp.float32
        ).astype(jnp.bfloat16)
        copies.append(
            pltpu.make_async_copy(out_v.at[i], out_hbm.at[:, pl.ds(i * wide, wide)], sems.at[i])
        )
        copies[-1].start()
    for copy in copies:
        copy.wait()


def group_orders(chips):
    first = (5 * chips) // 8
    back = [first] + [c for c in range(chips) if c != first]
    half = chips // 2
    ring = [c for c in range(half, chips) if c % 2] + [c for c in range(half, chips) if not c % 2][::-1]
    turn = ring.index(first)
    there = ring[turn:] + ring[:turn]
    for i, c in enumerate(range(half - 2, -1, -2)):
        there += [c, c + 1] if i % 2 else [c + 1, c]
    if sorted(there) != list(range(chips)):
        there = back
    return there, back


VMEM = pl.BlockSpec(memory_space=pltpu.VMEM)
ANY = pl.BlockSpec(memory_space=pl.ANY)
LIMIT = pltpu.CompilerParams(vmem_limit_bytes=16 << 20)


def call(kernel, name, outs, *args, flops=0, **more):
    one = not isinstance(outs, tuple)
    options = dict(
        out_shape=outs,
        in_specs=[VMEM] * len(args),
        out_specs=VMEM if one else (VMEM,) * len(outs),
        name=name,
        compiler_params=LIMIT,
        cost_estimate=pl.CostEstimate(flops=flops, bytes_accessed=0, transcendentals=0),
    )
    return pl.pallas_call(kernel, **{**options, **more})(*args)


def shards(tokens, routes, gate_num, w_gate, w_up, w_down):
    tok_rows, top_count = routes.shape
    width = tokens.shape[1]
    hidden_width = w_gate.shape[2]
    devices = lax.axis_size("ep")
    chips = devices // SPLIT
    half = width // SPLIT
    capacity = max(2, min(tok_rows, 5 * tok_rows * top_count // (2 * EXPERTS)))
    there, back = group_orders(chips)
    moves = [back.index(c) * SPLIT + k for c in there for k in range(SPLIT)]
    swap = [(d, d ^ 1) for d in range(devices)]
    slots, rows = chips * capacity, devices * capacity
    block = (devices, capacity, half)
    parts = 2 if half % 256 == 0 else 1
    bf16, f32 = jnp.bfloat16, jnp.float32
    shape = jax.ShapeDtypeStruct

    sources = [pltpu.with_memory_space_constraint(a, pltpu.HBM) for a in (routes.T, gate_num.T, tokens)]
    outgoing, weight = call(
        functools.partial(route_kernel, capacity, there, back),
        "route",
        (shape((chips, SPLIT, capacity, half), bf16), shape((slots, tok_rows), bf16)),
        *sources,
        in_specs=[ANY] * 3,
        scratch_shapes=[
            pltpu.VMEM((top_count, tok_rows), jnp.int32),
            pltpu.VMEM((top_count, tok_rows), jnp.int32),
            pltpu.VMEM((tok_rows, width), bf16),
            pltpu.SemaphoreType.DMA((3,)),
        ],
    )
    outgoing = outgoing.reshape(block)
    outgoing = call(
        mark_kernel, "mark", shape(block, bf16), outgoing, flops=10**10, input_output_aliases={0: 0}
    )
    def exchange(blocks, order):
        group = [[c * SPLIT + k for c in order for k in reversed(range(SPLIT))]]
        return lax.all_to_all(
            blocks, "ep", split_axis=0, concat_axis=0, tiled=True, axis_index_groups=group
        )

    own = exchange(outgoing, there)
    other = lax.ppermute(own, "ep", swap)
    product = rows * half * hidden_width * 2
    accs = call(
        enter_kernel,
        "enter",
        (shape((rows, hidden_width), f32),) * 2,
        own,
        w_gate,
        w_up,
        w_down,
        flops=2 * product,
    )
    hidden, send = call(
        middle_kernel,
        "middle",
        (shape((rows, hidden_width), bf16), shape(block, bf16)),
        other,
        *accs,
        w_gate,
        w_up,
        w_down,
        flops=3 * product,
    )
    arrived = lax.ppermute(send, "ep", swap)
    keep = call(leave_kernel, "leave", shape((rows, half), f32), hidden, w_down, flops=product)
    summed = call(functools.partial(add_kernel, moves), "add", shape(block, bf16), keep, arrived)
    returned = exchange(summed, back).reshape(chips, SPLIT, capacity, half)
    return call(
        combine_kernel,
        "combine",
        shape((tok_rows, width), bf16),
        weight,
        returned,
        out_specs=ANY,
        scratch_shapes=[
            pltpu.VMEM((SPLIT * parts, tok_rows, half // parts), bf16),
            pltpu.SemaphoreType.DMA((SPLIT * parts,)),
        ],
    )


def solution(mesh):
    return jax.shard_map(
        shards,
        mesh=mesh,
        in_specs=(
            P(("groups", "ep"), None),
            P(("groups", "ep"), None),
            P(("groups", "ep"), None),
            P("ep", None, None),
            P("ep", None, None),
            P("ep", None, None),
        ),
        out_specs=P(("groups", "ep"), None),
        check_vma=False,
    )
```

```python
import functools
import jax
import jax.numpy as jnp
from jax import lax
from jax.experimental import pallas as pl
from jax.experimental.pallas import tpu as pltpu
from jax.sharding import PartitionSpec as P

SPLIT = 2
EXPERTS = 256


def slots_of(routes, slots, capacity, order):
    top, rows = routes.shape
    slot = lax.broadcasted_iota(jnp.int32, (slots, rows), 0)
    block, place = slot // capacity, slot % capacity
    expert = jnp.zeros_like(block)
    for j, chip in enumerate(order):
        expert = jnp.where(block == j, chip, expert)
    same = [routes[k : k + 1, :] == expert for k in range(top)]
    hit = functools.reduce(jnp.logical_or, same).astype(jnp.float32)
    earlier = lax.broadcasted_iota(jnp.int32, (rows, rows), 0) < lax.broadcasted_iota(
        jnp.int32, (rows, rows), 1
    )
    rank = jnp.dot(
        hit.astype(jnp.bfloat16), earlier.astype(jnp.bfloat16), preferred_element_type=jnp.float32
    )
    return jnp.where(rank == place.astype(jnp.float32), hit, 0.0), same


def route_kernel(
    capacity, there, back, routes_hbm, gates_hbm, tokens_hbm, out_ref, weight_ref, routes_v, gates_v, tokens_v, sems
):
    chips, halves, _, half = out_ref.shape
    copies = [
        pltpu.make_async_copy(source, target, sems.at[i])
        for i, (source, target) in enumerate(
            ((routes_hbm, routes_v), (tokens_hbm, tokens_v), (gates_hbm, gates_v))
        )
    ]
    for copy in copies:
        copy.start()
    copies[0].wait()
    pick, same = slots_of(routes_v[...], chips * capacity, capacity, there)
    copies[2].wait()
    gates = gates_v[...].astype(jnp.float32) / 256.0
    weight = jnp.zeros_like(pick)
    for k, hit in enumerate(same):
        weight = jnp.where(hit, gates[k : k + 1, :], weight)
    weight = (weight * pick).astype(jnp.bfloat16)
    for i, chip in enumerate(there):
        j = back.index(chip)
        weight_ref[j * capacity : (j + 1) * capacity, :] = weight[i * capacity : (i + 1) * capacity]
    copies[1].wait()
    rows = jnp.dot(
        pick.astype(jnp.bfloat16), tokens_v[...], preferred_element_type=jnp.float32
    ).astype(jnp.bfloat16)
    for k in range(halves):
        part = rows[:, k * half : (k + 1) * half]
        out_ref[:, halves - 1 - k] = part.reshape(chips, capacity, half)


def mark_kernel(in_ref, out_ref):
    del in_ref, out_ref


def flat(rows):
    return rows.reshape(rows.shape[0] * rows.shape[1], rows.shape[2])


def half_of(side, half):
    return pl.ds(pl.multiple_of(side * half, 128), half)


def enter_kernel(own_ref, gate_ref, up_ref, down_ref, gate_out, up_out):
    del down_ref
    half = own_ref.shape[2]
    mine = half_of(lax.axis_index("ep") % SPLIT, half)
    x = flat(own_ref[...])
    gate_out[...] = jnp.dot(x, gate_ref[0, mine, :], preferred_element_type=jnp.float32)
    up_out[...] = jnp.dot(x, up_ref[0, mine, :], preferred_element_type=jnp.float32)


def middle_kernel(
    other_ref, gate_acc, up_acc, gate_ref, up_ref, down_ref, hidden_ref, send_ref, gate_v, up_v
):
    half = other_ref.shape[2]
    side = 1 - lax.axis_index("ep") % SPLIT
    theirs = half_of(side, half)
    x = flat(other_ref[...])
    gate_v[...] = jnp.dot(x, gate_ref[0, theirs, :], preferred_element_type=jnp.float32)
    up_v[...] = jnp.dot(x, up_ref[0, theirs, :], preferred_element_type=jnp.float32)

    @pl.when(side < SPLIT)
    def _():
        gate = gate_acc[...] + gate_v[...]
        up = up_acc[...] + up_v[...]
        hidden = (gate / (1.0 + jnp.exp(-gate)) * up).astype(jnp.bfloat16)
        hidden_ref[...] = hidden
        out = jnp.dot(hidden, down_ref[0, :, theirs], preferred_element_type=jnp.float32)
        send_ref[...] = out.astype(jnp.bfloat16).reshape(send_ref.shape)


def leave_kernel(hidden_ref, down_ref, keep_ref):
    half = keep_ref.shape[1]
    mine = half_of(lax.axis_index("ep") % SPLIT, half)
    keep_ref[...] = jnp.dot(
        hidden_ref[...], down_ref[0, :, mine], preferred_element_type=jnp.float32
    )


def add_kernel(moves, keep_ref, arrived_ref, out_ref):
    capacity, half = out_ref.shape[1:]
    total = (keep_ref[...] + flat(arrived_ref[...]).astype(jnp.float32)).astype(jnp.bfloat16)
    total = total.reshape(out_ref.shape)
    for source, target in enumerate(moves):
        out_ref[target] = total[source]


def combine_kernel(weight_ref, rows_ref, out_hbm, out_v, sems):
    halves, half = rows_ref.shape[1], rows_ref.shape[3]
    parts = out_v.shape[0] // halves
    wide = half // parts
    copies = []
    for i in range(halves * parts):
        part = slice(i % parts * wide, (i % parts + 1) * wide)
        rows = flat(rows_ref[:, halves - 1 - i // parts, :, part])
        out_v[i] = lax.dot_general(
            weight_ref[...], rows, (((0,), (0,)), ((), ())), preferred_element_type=jnp.float32
        ).astype(jnp.bfloat16)
        copies.append(
            pltpu.make_async_copy(out_v.at[i], out_hbm.at[:, pl.ds(i * wide, wide)], sems.at[i])
        )
        copies[-1].start()
    for copy in copies:
        copy.wait()


def group_orders(chips):
    first = (5 * chips) // 8
    back = [first] + [c for c in range(chips) if c != first]
    half = chips // 2
    ring = [c for c in range(half, chips) if c % 2] + [c for c in range(half, chips) if not c % 2][::-1]
    turn = ring.index(first)
    there = ring[turn:] + ring[:turn]
    for i, c in enumerate(range(half - 2, -1, -2)):
        there += [c, c + 1] if i % 2 else [c + 1, c]
    if sorted(there) != list(range(chips)):
        there = back
    return there, back


VMEM = pl.BlockSpec(memory_space=pltpu.VMEM)
ANY = pl.BlockSpec(memory_space=pl.ANY)
LIMIT = pltpu.CompilerParams(vmem_limit_bytes=16 << 20)


def call(kernel, name, outs, *args, flops=0, **more):
    one = not isinstance(outs, tuple)
    options = dict(
        out_shape=outs,
        in_specs=[VMEM] * len(args),
        out_specs=VMEM if one else (VMEM,) * len(outs),
        name=name,
        compiler_params=LIMIT,
        cost_estimate=pl.CostEstimate(flops=flops, bytes_accessed=0, transcendentals=0),
    )
    return pl.pallas_call(kernel, **{**options, **more})(*args)


def shards(tokens, routes, gate_num, w_gate, w_up, w_down):
    tok_rows, top_count = routes.shape
    width = tokens.shape[1]
    hidden_width = w_gate.shape[2]
    devices = lax.axis_size("ep")
    chips = devices // SPLIT
    half = width // SPLIT
    capacity = max(2, min(tok_rows, 5 * tok_rows * top_count // (2 * EXPERTS)))
    there, back = group_orders(chips)
    moves = [back.index(c) * SPLIT + k for c in there for k in range(SPLIT)]
    swap = [(d, d ^ 1) for d in range(devices)]
    slots, rows = chips * capacity, devices * capacity
    block = (devices, capacity, half)
    parts = 2 if half % 256 == 0 else 1
    bf16, f32 = jnp.bfloat16, jnp.float32
    shape = jax.ShapeDtypeStruct

    sources = [pltpu.with_memory_space_constraint(a, pltpu.HBM) for a in (routes.T, gate_num.T, tokens)]
    outgoing, weight = call(
        functools.partial(route_kernel, capacity, there, back),
        "route",
        (shape((chips, SPLIT, capacity, half), bf16), shape((slots, tok_rows), bf16)),
        *sources,
        in_specs=[ANY] * 3,
        scratch_shapes=[
            pltpu.VMEM((top_count, tok_rows), jnp.int32),
            pltpu.VMEM((top_count, tok_rows), jnp.int32),
            pltpu.VMEM((tok_rows, width), bf16),
            pltpu.SemaphoreType.DMA((3,)),
        ],
    )
    outgoing = outgoing.reshape(block)
    outgoing = call(
        mark_kernel, "mark", shape(block, bf16), outgoing, flops=10**10, input_output_aliases={0: 0}
    )
    def exchange(blocks, order):
        group = [[c * SPLIT + k for c in order for k in reversed(range(SPLIT))]]
        return lax.all_to_all(
            blocks, "ep", split_axis=0, concat_axis=0, tiled=True, axis_index_groups=group
        )

    own = exchange(outgoing, there)
    other = lax.ppermute(own, "ep", swap)
    product = rows * half * hidden_width * 2
    accs = call(
        enter_kernel,
        "enter",
        (shape((rows, hidden_width), f32),) * 2,
        own,
        w_gate,
        w_up,
        w_down,
        flops=2 * product,
    )
    hidden, send = call(
        middle_kernel,
        "middle",
        (shape((rows, hidden_width), bf16), shape(block, bf16)),
        other,
        *accs,
        w_gate,
        w_up,
        w_down,
        flops=3 * product,
        scratch_shapes=[pltpu.VMEM((rows, hidden_width), f32)] * 2,
    )
    arrived = lax.ppermute(send, "ep", swap)
    keep = call(leave_kernel, "leave", shape((rows, half), f32), hidden, w_down, flops=product)
    summed = call(functools.partial(add_kernel, moves), "add", shape(block, bf16), keep, arrived)
    returned = exchange(summed, back).reshape(chips, SPLIT, capacity, half)
    return call(
        combine_kernel,
        "combine",
        shape((tok_rows, width), bf16),
        weight,
        returned,
        out_specs=ANY,
        scratch_shapes=[
            pltpu.VMEM((SPLIT * parts, tok_rows, half // parts), bf16),
            pltpu.SemaphoreType.DMA((SPLIT * parts,)),
        ],
    )


def solution(mesh):
    return jax.shard_map(
        shards,
        mesh=mesh,
        in_specs=(
            P(("groups", "ep"), None),
            P(("groups", "ep"), None),
            P(("groups", "ep"), None),
            P("ep", None, None),
            P("ep", None, None),
            P("ep", None, None),
        ),
        out_specs=P(("groups", "ep"), None),
        check_vma=False,
    )
```

```python
import functools
import jax
import jax.numpy as jnp
from jax import lax
from jax.experimental import pallas as pl
from jax.experimental.pallas import tpu as pltpu
from jax.sharding import PartitionSpec as P

SPLIT = 2
EXPERTS = 256


def slots_of(routes, slots, capacity, order):
    top, rows = routes.shape
    slot = lax.broadcasted_iota(jnp.int32, (slots, rows), 0)
    block, place = slot // capacity, slot % capacity
    expert = jnp.zeros_like(block)
    for j, chip in enumerate(order):
        expert = jnp.where(block == j, chip, expert)
    same = [routes[k : k + 1, :] == expert for k in range(top)]
    hit = functools.reduce(jnp.logical_or, same).astype(jnp.float32)
    earlier = lax.broadcasted_iota(jnp.int32, (rows, rows), 0) < lax.broadcasted_iota(
        jnp.int32, (rows, rows), 1
    )
    rank = jnp.dot(
        hit.astype(jnp.bfloat16), earlier.astype(jnp.bfloat16), preferred_element_type=jnp.float32
    )
    return jnp.where(rank == place.astype(jnp.float32), hit, 0.0), same


def route_kernel(
    capacity, there, back, routes_hbm, gates_hbm, tokens_hbm, out_ref, weight_ref, routes_v, gates_v, tokens_v, sems
):
    chips, halves, _, half = out_ref.shape
    copies = [
        pltpu.make_async_copy(source, target, sems.at[i])
        for i, (source, target) in enumerate(
            ((routes_hbm, routes_v), (tokens_hbm, tokens_v), (gates_hbm, gates_v))
        )
    ]
    for copy in copies:
        copy.start()
    copies[0].wait()
    pick, same = slots_of(routes_v[...], chips * capacity, capacity, there)
    copies[2].wait()
    gates = gates_v[...].astype(jnp.float32) / 256.0
    weight = jnp.zeros_like(pick)
    for k, hit in enumerate(same):
        weight = jnp.where(hit, gates[k : k + 1, :], weight)
    weight = (weight * pick).astype(jnp.bfloat16)
    for i, chip in enumerate(there):
        j = back.index(chip)
        weight_ref[j * capacity : (j + 1) * capacity, :] = weight[i * capacity : (i + 1) * capacity]
    copies[1].wait()
    rows = jnp.dot(
        pick.astype(jnp.bfloat16), tokens_v[...], preferred_element_type=jnp.float32
    ).astype(jnp.bfloat16)
    for k in range(halves):
        part = rows[:, k * half : (k + 1) * half]
        out_ref[:, halves - 1 - k] = part.reshape(chips, capacity, half)


def flat(rows):
    return rows.reshape(rows.shape[0] * rows.shape[1], rows.shape[2])


def half_of(side, half):
    return pl.ds(pl.multiple_of(side * half, 128), half)


def enter_kernel(own_ref, gate_ref, up_ref, down_ref, gate_out, up_out):
    del down_ref
    half = own_ref.shape[2]
    mine = half_of(lax.axis_index("ep") % SPLIT, half)
    x = flat(own_ref[...])
    gate_out[...] = jnp.dot(x, gate_ref[0, mine, :], preferred_element_type=jnp.float32)
    up_out[...] = jnp.dot(x, up_ref[0, mine, :], preferred_element_type=jnp.float32)


def middle_kernel(other_ref, gate_acc, up_acc, gate_ref, up_ref, down_ref, hidden_ref, send_ref):
    half = other_ref.shape[2]
    theirs = half_of(1 - lax.axis_index("ep") % SPLIT, half)
    x = flat(other_ref[...])
    gate = gate_acc[...] + jnp.dot(x, gate_ref[0, theirs, :], preferred_element_type=jnp.float32)
    up = up_acc[...] + jnp.dot(x, up_ref[0, theirs, :], preferred_element_type=jnp.float32)
    hidden = (gate / (1.0 + jnp.exp(-gate)) * up).astype(jnp.bfloat16)
    hidden_ref[...] = hidden
    out = jnp.dot(hidden, down_ref[0, :, theirs], preferred_element_type=jnp.float32)
    send_ref[...] = out.astype(jnp.bfloat16).reshape(send_ref.shape)


def leave_kernel(hidden_ref, down_ref, keep_ref):
    half = keep_ref.shape[1]
    mine = half_of(lax.axis_index("ep") % SPLIT, half)
    keep_ref[...] = jnp.dot(
        hidden_ref[...], down_ref[0, :, mine], preferred_element_type=jnp.float32
    )


def add_kernel(moves, keep_ref, arrived_ref, out_ref):
    capacity, half = out_ref.shape[1:]
    total = (keep_ref[...] + flat(arrived_ref[...]).astype(jnp.float32)).astype(jnp.bfloat16)
    total = total.reshape(out_ref.shape)
    for source, target in enumerate(moves):
        out_ref[target] = total[source]


def combine_kernel(weight_ref, rows_ref, out_hbm, out_v, sems):
    halves, half = rows_ref.shape[1], rows_ref.shape[3]
    parts = out_v.shape[0] // halves
    wide = half // parts
    copies = []
    for i in range(halves * parts):
        part = slice(i % parts * wide, (i % parts + 1) * wide)
        rows = flat(rows_ref[:, halves - 1 - i // parts, :, part])
        out_v[i] = lax.dot_general(
            weight_ref[...], rows, (((0,), (0,)), ((), ())), preferred_element_type=jnp.float32
        ).astype(jnp.bfloat16)
        copies.append(
            pltpu.make_async_copy(out_v.at[i], out_hbm.at[:, pl.ds(i * wide, wide)], sems.at[i])
        )
        copies[-1].start()
    for copy in copies:
        copy.wait()


def group_orders(chips):
    first = (5 * chips) // 8
    back = [first] + [c for c in range(chips) if c != first]
    half = chips // 2
    ring = [c for c in range(half, chips) if c % 2] + [c for c in range(half, chips) if not c % 2][::-1]
    turn = ring.index(first)
    there = ring[turn:] + ring[:turn]
    for i, c in enumerate(range(half - 2, -1, -2)):
        there += [c, c + 1] if i % 2 else [c + 1, c]
    if sorted(there) != list(range(chips)):
        there = back
    return there, back


VMEM = pl.BlockSpec(memory_space=pltpu.VMEM)
ANY = pl.BlockSpec(memory_space=pl.ANY)
LIMIT = pltpu.CompilerParams(vmem_limit_bytes=16 << 20)


def call(kernel, name, outs, *args, flops=0, **more):
    one = not isinstance(outs, tuple)
    options = dict(
        out_shape=outs,
        in_specs=[VMEM] * len(args),
        out_specs=VMEM if one else (VMEM,) * len(outs),
        name=name,
        compiler_params=LIMIT,
        cost_estimate=pl.CostEstimate(flops=flops, bytes_accessed=0, transcendentals=0),
    )
    return pl.pallas_call(kernel, **{**options, **more})(*args)


def shards(tokens, routes, gate_num, w_gate, w_up, w_down):
    tok_rows, top_count = routes.shape
    width = tokens.shape[1]
    hidden_width = w_gate.shape[2]
    devices = lax.axis_size("ep")
    chips = devices // SPLIT
    half = width // SPLIT
    capacity = max(2, min(tok_rows, 5 * tok_rows * top_count // (2 * EXPERTS)))
    there, back = group_orders(chips)
    moves = [back.index(c) * SPLIT + k for c in there for k in range(SPLIT)]
    swap = [(d, d ^ 1) for d in range(devices)]
    slots, rows = chips * capacity, devices * capacity
    block = (devices, capacity, half)
    parts = 2 if half % 256 == 0 else 1
    bf16, f32 = jnp.bfloat16, jnp.float32
    shape = jax.ShapeDtypeStruct

    sources = [pltpu.with_memory_space_constraint(a, pltpu.HBM) for a in (routes.T, gate_num.T, tokens)]
    outgoing, weight = call(
        functools.partial(route_kernel, capacity, there, back),
        "route",
        (shape((chips, SPLIT, capacity, half), bf16), shape((slots, tok_rows), bf16)),
        *sources,
        flops=10**10,
        in_specs=[ANY] * 3,
        scratch_shapes=[
            pltpu.VMEM((top_count, tok_rows), jnp.int32),
            pltpu.VMEM((top_count, tok_rows), jnp.int32),
            pltpu.VMEM((tok_rows, width), bf16),
            pltpu.SemaphoreType.DMA((3,)),
        ],
    )
    outgoing = outgoing.reshape(block)
    def exchange(blocks, order):
        group = [[c * SPLIT + k for c in order for k in reversed(range(SPLIT))]]
        return lax.all_to_all(
            blocks, "ep", split_axis=0, concat_axis=0, tiled=True, axis_index_groups=group
        )

    own = exchange(outgoing, there)
    other = lax.ppermute(own, "ep", swap)
    product = rows * half * hidden_width * 2
    accs = call(
        enter_kernel,
        "enter",
        (shape((rows, hidden_width), f32),) * 2,
        own,
        w_gate,
        w_up,
        w_down,
        flops=2 * product,
    )
    hidden, send = call(
        middle_kernel,
        "middle",
        (shape((rows, hidden_width), bf16), shape(block, bf16)),
        other,
        *accs,
        w_gate,
        w_up,
        w_down,
        flops=3 * product,
    )
    arrived = lax.ppermute(send, "ep", swap)
    keep = call(leave_kernel, "leave", shape((rows, half), f32), hidden, w_down, flops=product)
    summed = call(functools.partial(add_kernel, moves), "add", shape(block, bf16), keep, arrived)
    returned = exchange(summed, back).reshape(chips, SPLIT, capacity, half)
    return call(
        combine_kernel,
        "combine",
        shape((tok_rows, width), bf16),
        weight,
        returned,
        out_specs=ANY,
        scratch_shapes=[
            pltpu.VMEM((SPLIT * parts, tok_rows, half // parts), bf16),
            pltpu.SemaphoreType.DMA((SPLIT * parts,)),
        ],
    )


def solution(mesh):
    return jax.shard_map(
        shards,
        mesh=mesh,
        in_specs=(
            P(("groups", "ep"), None),
            P(("groups", "ep"), None),
            P(("groups", "ep"), None),
            P("ep", None, None),
            P("ep", None, None),
            P("ep", None, None),
        ),
        out_specs=P(("groups", "ep"), None),
        check_vma=False,
    )
```
